32 devices in a mesh: tp: 8 (over y, x, core), dp: 4 (over z).
Axes of the slice: x: 2, y: 2, z: 4, core: 2. Of those that a mesh axis runs over, the one named last changes fastest.
Arguments:
- activations: bfloat16 [64, 512, 4096], P('dp', None, 'tp'), may hold values from -6 to 6
- query_output_cotangent: bfloat16 [64, 512, 4096], P('dp', None, 'tp'), may hold values from -6 to 6
- value_output_cotangent: bfloat16 [64, 512, 4096], P('dp', None, 'tp'), may hold values from -6 to 6
- lengths: int32 [64], P('dp'), may hold values from 1 to 512
- reducing_matrices_pair: bfloat16 [2, 4096, 128], P(None, 'tp'), may hold values from -0.09375 to 0.09375
- expanding_matrices_pair: bfloat16 [2, 128, 4096], P(None, None, 'tp'), may hold values from -0.5 to 0.5
- width_side_projections: bfloat16 [2, 4096, 128], P(None, 'tp'), may hold values from -0.09375 to 0.09375
- narrow_random_sketch: bfloat16 [128, 16], replicated, may hold values from -0.5 to 0.5
- projected_first_moment: float32 [8192], replicated, may hold values from -6 to 6
- projected_second_moment: float32 [8192], replicated, may hold values from 0.1 to 10
- targets: bfloat16 [1024, 8192], P('dp', 'tp'), may hold values from -6 to 6
Outputs:
- scores: float32 [64, 1024], P('dp', 'tp')
The draws below stay inside these ranges and needn't reach their ends.
All inputs are finite; a program needn't handle non-finite values.
Results may differ from the reference program's by a relative error of at most 0.023.
Values may be sent and summed in bfloat16 or wider, within the bound.
A program may use at most 128 MiB of HBM per device.

```python
import math
import jax
import jax.numpy as jnp
from jax import lax

HIDDEN_SIZE = 4096
LOW_DIMENSION = 128
KD = 128
SKETCH_LOW_COORD = 16
SEQ = 512
EVAL_CASES = 1024
K = 8192
DSH = 512
WIN = 64
N_TP = 8


def with_ends(values, rng, least, top_value):
    spot = [jax.random.randint(jax.random.fold_in(rng, axis), (), 0, length) for axis, length in enumerate(values.shape)]
    widest = values.shape.index(max(values.shape))
    neighbour = spot[:widest] + [(spot[widest] + 1) % values.shape[widest]] + spot[widest + 1:]
    return values.at[tuple(spot)].set(least).at[tuple(neighbour)].set(top_value)


def steps_of(key, shape, cuts, least, largest):
    gain, own = 1.0, jax.random.fold_in(key, 6)
    for dim, blocks in cuts:
        heights = jnp.exp(jax.random.uniform(jax.random.fold_in(own, dim), (blocks,), jnp.float32, least / len(cuts), largest / len(cuts)))
        gain = gain * jnp.repeat(heights, shape[dim] // blocks).reshape([-1 if axis == dim else 1 for axis in range(len(shape))])
    return gain


def noise(key, extent, deviation, most, split=(), held_as=jnp.bfloat16):
    result = deviation * jax.random.normal(key, extent, jnp.float32)
    if split:
        result = result * steps_of(key, extent, split, -0.22, 0.18)
    return jnp.clip(result, -most, most).astype(held_as)


def setup_inputs(seed: int = 0) -> dict:
    key_list = jax.random.split(jax.random.key(seed), 12)
    return {
        "activations": noise(key_list[0], (WIN, SEQ, HIDDEN_SIZE), 1.0, 6.0, ((0, 4), (2, 8))),
        "query_output_cotangent": noise(key_list[1], (WIN, SEQ, HIDDEN_SIZE), 1.0, 6.0, ((0, 4), (2, 8))),
        "value_output_cotangent": noise(key_list[2], (WIN, SEQ, HIDDEN_SIZE), 1.0, 6.0, ((0, 4), (2, 8))),
        "lengths": with_ends(jax.random.randint(key_list[3], (WIN,), 1, SEQ + 1), jax.random.fold_in(key_list[3], 1), 1, SEQ).astype(jnp.int32),
        "reducing_matrices_pair": noise(key_list[4], (2, HIDDEN_SIZE, LOW_DIMENSION), HIDDEN_SIZE ** -0.5, 0.09375, ((1, 8),)),
        "expanding_matrices_pair": noise(key_list[5], (2, LOW_DIMENSION, HIDDEN_SIZE), LOW_DIMENSION ** -0.5, 0.5, ((2, 8),)),
        "width_side_projections": noise(key_list[6], (2, HIDDEN_SIZE, KD), HIDDEN_SIZE ** -0.5, 0.09375, ((1, 8),)),
        "narrow_random_sketch": noise(key_list[7], (LOW_DIMENSION, SKETCH_LOW_COORD), LOW_DIMENSION ** -0.5, 0.5),
        "projected_first_moment": noise(key_list[8], (K,), 1.0, 6.0, (), jnp.float32),
        "projected_second_moment": jnp.clip(jnp.exp(jax.random.uniform(key_list[9], (K,), jnp.float32, math.log(0.1), math.log(10.0))), 0.1, 10.0),
        "targets": noise(key_list[10], (EVAL_CASES, K), 1.0, 6.0, ((0, 4), (1, 8))),
    }


def compute_features(token_sums, token_mask, layout, rank_cols):
    wide_cols = (token_sums.shape[-1] - 4 * rank_cols) // 3
    bounds = [0, rank_cols, 2 * rank_cols, 2 * rank_cols + wide_cols, 3 * rank_cols + wide_cols, 3 * rank_cols + 2 * wide_cols, 4 * rank_cols + 2 * wide_cols, 4 * rank_cols + 3 * wide_cols]
    pieces = [token_sums[..., bounds[i]:bounds[i + 1]] for i in range(7)]
    down_q, down_v, input_side, back_q, output_q, back_v, output_v = pieces
    weights = token_mask[..., None]
    pattern = layout + 'r,' + layout + 'k->erk'

    def outer_sum(left_side, right_side):
        return jnp.einsum(pattern, left_side, right_side, precision=lax.Precision.HIGHEST)
    stacked = jnp.stack([outer_sum(back_q * weights, input_side), outer_sum(back_v * weights, input_side), outer_sum(down_q * weights, output_q), outer_sum(down_v * weights, output_v)], axis=1)
    return stacked.reshape(stacked.shape[0], -1)

def adam_update(features, first_moment, second_moment):
    mixed = 0.9 * first_moment + 0.1 * features
    spread = 0.999 * second_moment + 0.001 * features * features
    return mixed / (jnp.sqrt(spread) + 1e-08)

def combine_factors(reducing_matrices_pair, expanding_matrices_pair, narrow_random_sketch):
    attention_key_reducer = jnp.dot(reducing_matrices_pair[0], narrow_random_sketch, preferred_element_type=jnp.float32).astype(jnp.bfloat16)
    value_down_factor = jnp.dot(reducing_matrices_pair[1], narrow_random_sketch, preferred_element_type=jnp.float32).astype(jnp.bfloat16)
    query_up_factor = jnp.dot(expanding_matrices_pair[0].T, narrow_random_sketch, preferred_element_type=jnp.float32).astype(jnp.bfloat16)
    value_up_factor = jnp.dot(expanding_matrices_pair[1].T, narrow_random_sketch, preferred_element_type=jnp.float32).astype(jnp.bfloat16)
    return (attention_key_reducer, value_down_factor, query_up_factor, value_up_factor)

def reference(activations, query_output_cotangent, value_output_cotangent, lengths, reducing_matrices_pair, expanding_matrices_pair, width_side_projections, narrow_random_sketch, projected_first_moment, projected_second_moment, targets):
    attention_key_reducer, value_down_factor, query_up_factor, value_up_factor = combine_factors(reducing_matrices_pair, expanding_matrices_pair, narrow_random_sketch)
    rank_cols = narrow_random_sketch.shape[1]
    w_left = jnp.concatenate([attention_key_reducer, value_down_factor, width_side_projections[0]], axis=1)
    w_query = jnp.concatenate([query_up_factor, width_side_projections[1]], axis=1)
    w_value = jnp.concatenate([value_up_factor, width_side_projections[1]], axis=1)
    left_groups = w_left.astype(jnp.float32).reshape(N_TP, DSH, -1)
    query_groups = w_query.astype(jnp.float32).reshape(N_TP, DSH, -1)
    value_groups = w_value.astype(jnp.float32).reshape(N_TP, DSH, -1)

    def grouped(rows, weights):
        split_rows = rows.astype(jnp.float32).reshape(SEQ, N_TP, DSH)
        parts = jnp.einsum('sgd,gdc->gsc', split_rows, weights, precision=lax.Precision.HIGHEST)
        rounded = lax.optimization_barrier(parts.astype(jnp.bfloat16)).astype(jnp.float32)
        return lax.optimization_barrier(jnp.sum(rounded, axis=0))

    def one_example(items):
        rows_x, rows_q, rows_v, length = items
        token_sums = jnp.concatenate([grouped(rows_x, left_groups), grouped(rows_q, query_groups), grouped(rows_v, value_groups)], axis=-1)
        token_mask = (jnp.arange(SEQ, dtype=jnp.int32) < length).astype(jnp.float32)
        return compute_features(token_sums[None], token_mask[None], 'es', rank_cols)[0]
    features = lax.map(one_example, (activations, query_output_cotangent, value_output_cotangent, lengths))
    update = adam_update(features, projected_first_moment, projected_second_moment)
    train_rows = (update * lax.rsqrt(lax.optimization_barrier(jnp.sum(update * update, axis=1)) + 1e-06)[:, None]).astype(jnp.bfloat16)
    target_float = targets.astype(jnp.float32)
    unit_targets = (target_float * lax.rsqrt(lax.optimization_barrier(jnp.sum(target_float * target_float, axis=1)) + 1e-06)[:, None]).astype(jnp.bfloat16)
    scores = jnp.dot(train_rows, unit_targets.T, preferred_element_type=jnp.float32)
    return scores * math.sqrt(K)
```

```python
import functools
import math

import jax
import jax.numpy as jnp
from jax import lax
from jax.experimental import pallas as pl
from jax.experimental.pallas import tpu as pltpu
from jax.sharding import PartitionSpec as P

MESH = pl.DeviceIdType.MESH
F32 = jnp.float32
BF16 = jnp.bfloat16
PARTS = 2
LAG = 3


def mm(a, b, ca=1, cb=0):
    return lax.dot_general(a, b, (((ca,), (cb,)), ((), ())), preferred_element_type=F32)


def kernel(
    nd,
    n,
    x_hbm,
    q_hbm,
    v_hbm,
    len_ref,
    red_hbm,
    exp_hbm,
    width_hbm,
    sketch_ref,
    m1_ref,
    m2_ref,
    t_hbm,
    out_ref,
    x_buf,
    q_buf,
    v_buf,
    t_buf,
    red_ref,
    exp_ref,
    w_buf,
    wide_out,
    wide_in,
    wide_own,
    pair_out,
    pair_in,
    mine,
    comb,
    step_in,
    found,
    feat_out,
    feat_in,
    u_all,
    u_f32,
    sq_out,
    sq_in,
    t_out,
    t_in,
    g_out,
    g_in,
    load_sem,
    t_sem,
    fixed_sem,
    pair_s,
    pair_r,
    wide_s,
    wide_r,
    step_s,
    step_r,
    feat_s,
    feat_r,
    u_s,
    u_r,
    sq_s,
    sq_r,
    tn_s,
    tn_r,
    g_s,
    g_r,
    low_sem,
    high_sem,
):
    d = lax.axis_index("dp")
    c = lax.axis_index("tp")
    chips = n // 2
    levels = chips.bit_length() - 1
    chip, core = c // 2, lax.rem(c, 2)
    partner = chip * 2 + 1 - core
    examples, seq, depth = x_buf.shape
    pairs = examples // 2
    rc = sketch_ref.shape[0]
    ranks = 4 * rc
    half = seq // 2
    rows = ranks // n
    batches, _, tile, _ = feat_out.shape
    per = tile // rows
    own_targets = t_buf.shape[0]
    out_cols = out_ref.shape[1]
    piece = min(own_targets, out_cols)
    halves = own_targets // piece
    slots = out_cols // piece
    last_lag = 1 + LAG * levels

    def remote(src, dst, send, recv, dd, cc):
        return pltpu.make_async_remote_copy(
            src_ref=src, dst_ref=dst, send_sem=send, recv_sem=recv, device_id={"dp": dd, "tp": cc}, device_id_type=MESH
        )

    def signal(sem, dd, cc):
        pl.semaphore_signal(sem, inc=1, device_id={"dp": dd, "tp": cc}, device_id_type=MESH)

    def across(bit):
        m = 1 << bit
        return (chip + m * (1 - 2 * lax.rem(chip // m, 2))) * 2 + core

    barrier = pltpu.get_barrier_semaphore()
    signal(barrier, d, partner)
    for bit in range(levels):
        signal(barrier, d, across(bit))

    @pl.when(d > 0)
    def _():
        signal(barrier, d - 1, c)

    @pl.when(d < nd - 1)
    def _():
        signal(barrier, d + 1, c)

    def load(e):
        return [
            pltpu.make_async_copy(src.at[e], dst.at[e], load_sem.at[j, e])
            for j, (src, dst) in enumerate(((x_hbm, x_buf), (q_hbm, q_buf), (v_hbm, v_buf)))
        ]

    def start_loads(i, _):
        for e in ((1 - core) * pairs + i, core * pairs + i):
            for copy in load(e):
                copy.start()
        return 0

    fixed = [
        pltpu.make_async_copy(src, dst, fixed_sem.at[j])
        for j, (src, dst) in enumerate(
            [(red_hbm, red_ref), (exp_hbm, exp_ref)]
            + [(width_hbm.at[min(j, 1)], w_buf.at[j, :, 128:]) for j in range(3)]
        )
    ]
    for copy in fixed:
        copy.start()
    lax.fori_loop(0, pairs, start_loads, 0)
    t_copy = pltpu.make_async_copy(t_hbm, t_buf, t_sem)
    t_copy.start()

    sketch = sketch_ref[...]

    def placed(slot):
        row = lax.broadcasted_iota(jnp.int32, (rc, 128), 0)
        col = lax.broadcasted_iota(jnp.int32, (rc, 128), 1)
        here = jnp.logical_or(col == row + slot * rc, col == row + slot * rc + ranks)
        return mm(sketch, jnp.where(here, 1.0, 0.0).astype(BF16), 0, 0).astype(BF16)

    spread = [placed(slot) for slot in range(4)]
    fixed[0].wait()
    w_buf[0, :, :128] = (mm(red_ref[0], spread[2]) + mm(red_ref[1], spread[3])).astype(BF16)
    fixed[1].wait()
    w_buf[1, :, :128] = mm(exp_ref[0], spread[0], 0, 0).astype(BF16)
    w_buf[2, :, :128] = mm(exp_ref[1], spread[1], 0, 0).astype(BF16)
    for copy in fixed[2:]:
        copy.wait()

    lower, upper_plane = jnp.where(d > 0, 1, 0), jnp.where(d < nd - 1, 1, 0)
    pl.semaphore_wait(barrier, 1 + levels + lower + upper_plane)

    def tell():
        @pl.when(d > 0)
        def _():
            signal(high_sem, d - 1, c)

        @pl.when(d < nd - 1)
        def _():
            signal(low_sem, d + 1, c)

    def hear():
        @pl.when(d > 0)
        def _():
            pl.semaphore_wait(low_sem, 1)

        @pl.when(d < nd - 1)
        def _():
            pl.semaphore_wait(high_sem, 1)

    if nd > 2:
        tell()

    def project(e, wide, i, out):
        row = lax.broadcasted_iota(jnp.int32, (half, 128), 0)
        upper = lax.broadcasted_iota(jnp.int32, (half, 128), 1) >= ranks
        live = jnp.where(upper, row + half, row) < len_ref[e]
        for k in range(half // 128):
            sums = []
            for late in range(2):
                span = pl.ds(late * half + k * 128, 128)
                narrow = None
                for j, buf in enumerate((x_buf, q_buf, v_buf)):
                    res = mm(buf[e, span], w_buf[j])
                    wide[i, span, j * 128 : (j + 1) * 128] = res[:, 128:].astype(BF16)
                    narrow = res[:, :128] if narrow is None else narrow + res[:, :128]
                sums.append(narrow)
            packed = jnp.where(upper[:128], sums[1], sums[0])
            packed = jnp.where(live[k * 128 : (k + 1) * 128], packed, 0.0).astype(BF16)
            out[i, :, :, k * 128 : (k + 1) * 128] = packed.T.reshape(PARTS, ranks, 128)

    def pair_copy(i):
        return remote(pair_out.at[i], pair_in.at[i], pair_s.at[i], pair_r.at[i], d, partner)

    def wide_copy(i):
        return remote(wide_out.at[i], wide_in.at[i], wide_s.at[i], wide_r.at[i], d, partner)

    def step_copy(i, level, part):
        return remote(
            comb.at[i, level, part],
            step_in.at[i, level, part],
            step_s.at[i, level, part],
            step_r.at[i, level, part],
            d,
            across((level + part) % levels),
        )

    def feat_copy(b, r):
        to = lax.rem(c + r, n)
        return remote(feat_out.at[b, to], feat_in.at[b, r], feat_s.at[b, r], feat_r.at[b, r], d, to)

    def u_copy(b, r, place):
        to = lax.rem(d + r, nd)
        return remote(u_all.at[b, place], u_all.at[b, place], u_s.at[b, r], u_r.at[b, r], to, c)

    def sq_copy(r):
        to = lax.rem(c + r, n)
        return remote(sq_out, sq_in.at[r], sq_s.at[r], sq_r.at[r], d, to)

    def home(h):
        return (d * own_targets + h * piece) // out_cols, lax.rem(d * own_targets + h * piece, out_cols) // piece

    def t_copy_out(i, h):
        j, s = home(h)
        return remote(t_out.at[h], t_in.at[s, c], tn_s.at[i, h], tn_r.at[s, c], i, j)

    def g_copy(i, h):
        j, s = home(h)
        return remote(g_out.at[i, h], g_in.at[s, c], g_s.at[i, h], g_r.at[s, c], i, j)

    def scatter_pieces(make, own_in, own_out):
        for i in range(nd):
            for h in range(halves):
                j, s = home(h)
                here = jnp.logical_and(d == i, c == j)

                @pl.when(jnp.logical_not(here))
                def _():
                    make(i, h).start()

                @pl.when(here)
                def _():
                    own_in[s, c] = own_out(i, h)

    def drain_pieces(make):
        for i in range(nd):
            for h in range(halves):
                j, _ = home(h)

                @pl.when(jnp.logical_not(jnp.logical_and(d == i, c == j)))
                def _():
                    make(i, h).wait_send()

    def receive_pieces(buf, send, recv):
        for s in range(slots):
            source = (c * out_cols + s * piece) // own_targets
            for cc in range(n):

                @pl.when(jnp.logical_not(jnp.logical_and(d == source, c == cc)))
                def _():
                    block = buf.at[s, cc]
                    remote(block, block, send.at[0, 0], recv.at[s, cc], source, cc).wait_recv()

    def turn(it, lag):
        return jnp.logical_and(it >= lag, it < pairs + lag)

    def step(it, _):
        @pl.when(it < pairs)
        def _():
            for e in ((1 - core) * pairs + it, core * pairs + it):
                for copy in load(e):
                    copy.wait()
            project((1 - core) * pairs + it, wide_out, it, pair_out)
            project(core * pairs + it, wide_own, it, mine)
            pair_copy(it).start()
            wide_copy(it).start()

        @pl.when(turn(it, 1))
        def _():
            i = it - 1
            pair_copy(i).wait_recv()
            for part in range(PARTS):
                comb[i, 0, part] = (mine[i, part].astype(F32) + pair_in[i, part].astype(F32)).astype(BF16)
                step_copy(i, 0, part).start()

        for level in range(1, levels):

            @pl.when(turn(it, 1 + LAG * level))
            def _():
                i = it - (1 + LAG * level)
                for part in range(PARTS):
                    step_copy(i, level - 1, part).wait_recv()
                    both = comb[i, level - 1, part].astype(F32) + step_in[i, level - 1, part].astype(F32)
                    comb[i, level, part] = both.astype(BF16)
                    step_copy(i, level, part).start()

        @pl.when(turn(it, last_lag))
        def _():
            i = it - last_lag
            wide_copy(i).wait_recv()
            whole = []
            for part in range(PARTS):
                step_copy(i, levels - 1, part).wait_recv()
                both = comb[i, levels - 1, part].astype(F32) + step_in[i, levels - 1, part].astype(F32)
                whole.append(both.astype(BF16))
            g = jnp.concatenate(whole, axis=1)
            left = mm(g, wide_own[i, :, :256]) + mm(g, wide_in[i, :, :256])
            right = mm(g[3 * rc :], wide_own[i, :, 256:]) + mm(g[3 * rc :], wide_in[i, :, 256:])
            b, place = i // per, lax.rem(i, per)
            found[place, : 2 * rc] = left[: 2 * rc, :128]
            found[place, 2 * rc : 3 * rc] = left[2 * rc : 3 * rc, 128:]
            found[place, 3 * rc :] = right

            @pl.when(place == per - 1)
            def _():
                for q in range(n):
                    feat_out[b, q] = jnp.concatenate(
                        [found[p, q * rows : (q + 1) * rows] for p in range(per)], axis=0
                    ).astype(BF16)
                for r in range(1, n):
                    feat_copy(b, r).start()

        if nd > 2:

            @pl.when(jnp.logical_and(lax.rem(it, 2) == 0, jnp.logical_and(it >= 2, it <= 2 * (nd - 2))))
            def _():
                hear()

                @pl.when(it < 2 * (nd - 2))
                def _():
                    tell()

        @pl.when(it == pairs)
        def _():
            t_copy.wait()
            t = t_buf[...].astype(F32)
            norm = jnp.broadcast_to(jnp.sum(t * t, axis=1, keepdims=True), (own_targets, 128)).T
            for h in range(halves):
                t_out[h] = norm[:8, h * piece : (h + 1) * piece]

        return 0

    lax.fori_loop(0, max(pairs + last_lag, 2 * (nd - 2) + 1), step, 0)

    m1 = jnp.concatenate([m1_ref[c]] * per, axis=0)
    m2 = jnp.concatenate([m2_ref[c]] * per, axis=0)

    def keep(b, i, k, u):
        u = u.astype(F32)
        for p in range(per):
            u_f32[i * examples + k * pairs + b * per + p] = u[p * rows : (p + 1) * rows]

    for b in range(batches):
        sums = [feat_out[b, c].astype(F32), None]
        for r in range(1, n):
            feat_copy(b, r).wait_recv()
            f = feat_in[b, r].astype(F32)
            sums[r % 2] = f if sums[r % 2] is None else sums[r % 2] + f
        for f, k in ((sums[0], core), (sums[1], 1 - core)):
            new = (0.9 * m1 + 0.1 * f) / (jnp.sqrt(0.999 * m2 + 0.001 * f * f) + 1e-08)
            u = new.astype(BF16)
            u_all[b, d, k] = u
            keep(b, d, k, u)
        for r in range(1, nd):
            u_copy(b, r, d).start()

    squares = None
    for r in range(rows):
        u = u_f32[pl.ds(d * examples, examples), r, :]
        squares = u * u if squares is None else squares + u * u
    sq_out[...] = squares
    for r in range(1, n):
        sq_copy(r).start()

    for b in range(batches):
        for r in range(1, nd):
            source = lax.rem(d + nd - r, nd)
            u_copy(b, r, source).wait_recv()
            for k in range(2):
                keep(b, source, k, u_all[b, source, k])
        if b == 0:
            scatter_pieces(t_copy_out, t_in, lambda i, h: t_out[h])

    u_rows = jnp.concatenate([u_f32[:, r, :].astype(BF16) for r in range(rows)], axis=1)
    dots = mm(u_rows, t_buf[...], 1, 1).astype(BF16)
    for i in range(nd):
        for h in range(halves):
            g_out[i, h] = dots[i * examples : (i + 1) * examples, h * piece : (h + 1) * piece]
    scatter_pieces(g_copy, g_in, lambda i, h: g_out[i, h])

    for r in range(1, n):
        sq_copy(r).wait_recv()
        squares = squares + sq_in[r]
    row_scale = lax.rsqrt(jnp.sum(squares, axis=1, keepdims=True) + 1e-06) * math.sqrt(ranks * 128)
    receive_pieces(t_in, tn_s, tn_r)
    column_scale = []
    for s in range(slots):
        norm = t_in[s, 0]
        for cc in range(1, n):
            norm = norm + t_in[s, cc]
        column_scale.append(lax.rsqrt(norm[:1] + 1e-06))
    receive_pieces(g_in, g_s, g_r)
    for s in range(slots):
        acc = g_in[s, 0].astype(F32)
        for cc in range(1, n):
            acc = acc + g_in[s, cc].astype(F32)
        out_ref[:, s * piece : (s + 1) * piece] = acc * row_scale * column_scale[s]

    def drain(i, _):
        pair_copy(i).wait_send()
        wide_copy(i).wait_send()
        for level in range(levels):
            for part in range(PARTS):
                step_copy(i, level, part).wait_send()
        return 0

    lax.fori_loop(0, pairs, drain, 0)
    for b in range(batches):
        for r in range(1, n):
            feat_copy(b, r).wait_send()
        for r in range(1, nd):
            u_copy(b, r, d).wait_send()
    for r in range(1, n):
        sq_copy(r).wait_send()
    drain_pieces(t_copy_out)
    drain_pieces(g_copy)


def body(nd, n, x, q, v, lengths, reducing, expanding, width, sketch, m1, m2, targets):
    examples, seq, depth = x.shape
    ranks = 4 * sketch.shape[1]
    pairs, chips, rows = examples // 2, n // 2, ranks // n
    levels = chips.bit_length() - 1
    half = seq // 2
    per = max(1, 16 // rows)
    batches = pairs // per
    own_targets = targets.shape[0]
    out_cols = own_targets * nd // n
    piece = min(own_targets, out_cols)
    halves, slots = own_targets // piece, out_cols // piece
    dma = pltpu.SemaphoreType.DMA
    anywhere = pl.BlockSpec(memory_space=pl.ANY)
    vmem = pl.BlockSpec(memory_space=pltpu.VMEM)
    smem = pl.BlockSpec(memory_space=pltpu.SMEM)
    return pl.pallas_call(
        functools.partial(kernel, nd, n),
        out_shape=jax.ShapeDtypeStruct((examples, out_cols), F32),
        in_specs=[anywhere] * 3 + [smem] + [anywhere] * 3 + [vmem] * 3 + [anywhere],
        out_specs=vmem,
        scratch_shapes=[
            pltpu.VMEM((examples, seq, depth), BF16),
            pltpu.VMEM((examples, seq, depth), BF16),
            pltpu.VMEM((examples, seq, depth), BF16),
            pltpu.VMEM(targets.shape, BF16),
            pltpu.VMEM(reducing.shape, BF16),
            pltpu.VMEM(expanding.shape, BF16),
            pltpu.VMEM((3, depth, 256), BF16),
            pltpu.VMEM((pairs, seq, 384), BF16),
            pltpu.VMEM((pairs, seq, 384), BF16),
            pltpu.VMEM((pairs, seq, 384), BF16),
            pltpu.VMEM((pairs, PARTS, ranks, half), BF16),
            pltpu.VMEM((pairs, PARTS, ranks, half), BF16),
            pltpu.VMEM((pairs, PARTS, ranks, half), BF16),
            pltpu.VMEM((pairs, levels, PARTS, ranks, half), BF16),
            pltpu.VMEM((pairs, levels, PARTS, ranks, half), BF16),
            pltpu.VMEM((per, ranks, 128), F32),
            pltpu.VMEM((batches, n, per * rows, 128), BF16),
            pltpu.VMEM((batches, n, per * rows, 128), BF16),
            pltpu.VMEM((batches, nd, 2, per * rows, 128), BF16),
            pltpu.VMEM((nd * examples, rows, 128), F32),
            pltpu.VMEM((examples, 128), F32),
            pltpu.VMEM((n, examples, 128), F32),
            pltpu.VMEM((halves, 8, piece), F32),
            pltpu.VMEM((slots, n, 8, piece), F32),
            pltpu.VMEM((nd, halves, examples, piece), BF16),
            pltpu.VMEM((slots, n, examples, piece), BF16),
            dma((3, examples)),
            dma,
            dma((5,)),
            dma((pairs,)),
            dma((pairs,)),
            dma((pairs,)),
            dma((pairs,)),
            dma((pairs, levels, PARTS)),
            dma((pairs, levels, PARTS)),
            dma((batches, n)),
            dma((batches, n)),
            dma((batches, nd)),
            dma((batches, nd)),
            dma((n,)),
            dma((n,)),
            dma((nd, halves)),
            dma((slots, n)),
            dma((nd, halves)),
            dma((slots, n)),
            pltpu.SemaphoreType.REGULAR,
            pltpu.SemaphoreType.REGULAR,
        ],
        compiler_params=pltpu.CompilerParams(
            collective_id=0, has_side_effects=True, vmem_limit_bytes=56 * 1024 * 1024
        ),
    )(
        x,
        q,
        v,
        lengths,
        reducing,
        expanding,
        width,
        sketch.T,
        m1.reshape(n, rows, 128),
        m2.reshape(n, rows, 128),
        targets,
    )


def solution(mesh):
    placed = (
        P("dp", None, "tp"),
        P("dp", None, "tp"),
        P("dp", None, "tp"),
        P("dp"),
        P(None, "tp", None),
        P(None, None, "tp"),
        P(None, "tp", None),
        P(),
        P(),
        P(),
        P("dp", "tp"),
    )
    names = mesh.axis_names
    order = (mesh.shape["dp"], mesh.shape["tp"])
    run = functools.partial(body, *order)
    assert set(names) == {"dp", "tp"}
    return jax.shard_map(run, mesh=mesh, in_specs=placed, out_specs=P("dp", "tp"), check_vma=False)
```

```python
import functools
import math

import jax
import jax.numpy as jnp
from jax import lax
from jax.experimental import pallas as pl
from jax.experimental.pallas import tpu as pltpu
from jax.sharding import PartitionSpec as P

MESH = pl.DeviceIdType.MESH
F32 = jnp.float32
BF16 = jnp.bfloat16
PARTS = 2
LAG = 3


def mm(a, b, ca=1, cb=0):
    return lax.dot_general(a, b, (((ca,), (cb,)), ((), ())), preferred_element_type=F32)


def kernel(
    nd,
    n,
    x_hbm,
    q_hbm,
    v_hbm,
    len_hbm,
    red_hbm,
    exp_hbm,
    width_hbm,
    sketch_hbm,
    m1_hbm,
    m2_hbm,
    t_hbm,
    out_ref,
    in_buf,
    t_buf,
    len_ref,
    sketch_ref,
    m_ref,
    red_ref,
    exp_ref,
    w_buf,
    wide_out,
    wide_in,
    wide_own,
    pair_out,
    pair_in,
    mine,
    comb,
    step_in,
    found,
    feat_out,
    feat_in,
    u_all,
    u_f32,
    sq_out,
    sq_in,
    t_out,
    t_in,
    g_out,
    g_in,
    load_sem,
    t_sem,
    fixed_sem,
    send_sem,
    pair_r,
    wide_r,
    step_r,
    feat_r,
    u_r,
    sq_r,
    tn_s,
    tn_r,
    g_s,
    g_r,
    low_sem,
    high_sem,
):
    d = lax.axis_index("dp")
    c = lax.axis_index("tp")
    chips = n // 2
    levels = chips.bit_length() - 1
    chip, core = c // 2, lax.rem(c, 2)
    partner = chip * 2 + 1 - core
    pairs, _, _, seq, depth = in_buf.shape
    examples = pairs * 2
    rc = sketch_ref.shape[0]
    ranks = 4 * rc
    half = seq // 2
    rows = ranks // n
    batches, _, tile, _ = feat_out.shape
    per = tile // rows
    own_targets = t_buf.shape[0]
    out_cols = out_ref.shape[1]
    piece = min(own_targets, out_cols)
    halves = own_targets // piece
    slots = out_cols // piece
    last_lag = 1 + LAG * levels

    def remote(src, dst, send, recv, dd, cc):
        return pltpu.make_async_remote_copy(
            src_ref=src, dst_ref=dst, send_sem=send, recv_sem=recv, device_id={"dp": dd, "tp": cc}, device_id_type=MESH
        )

    def arrived(block, sem):
        pltpu.make_async_copy(block, block, sem).wait()

    def received(block, sem):
        remote(block, block, sem, sem, d, partner).wait_recv()

    def sent(block, sem):
        remote(block, block, sem, sem, d, partner).wait_send()

    def signal(sem, dd, cc):
        pl.semaphore_signal(sem, inc=1, device_id={"dp": dd, "tp": cc}, device_id_type=MESH)

    def across(bit):
        m = 1 << bit
        return (chip + m * (1 - 2 * lax.rem(chip // m, 2))) * 2 + core

    barrier = pltpu.get_barrier_semaphore()
    signal(barrier, d, partner)
    for bit in range(levels):
        signal(barrier, d, across(bit))

    @pl.when(d > 0)
    def _():
        signal(barrier, d - 1, c)

    @pl.when(d < nd - 1)
    def _():
        signal(barrier, d + 1, c)

    fixed = [
        pltpu.make_async_copy(src, dst, fixed_sem.at[j])
        for src, dst, j in [(sketch_hbm, sketch_ref, 0), (red_hbm, red_ref, 1), (exp_hbm, exp_ref, 2)]
        + [(width_hbm.at[min(j, 1)], w_buf.at[j, :, 128:], 3) for j in range(3)]
        + [(len_hbm, len_ref, 4), (m1_hbm, m_ref.at[0], 5), (m2_hbm, m_ref.at[1], 5)]
    ]
    for copy in fixed:
        copy.start()

    def start_loads(i, _):
        for side in range(2):
            e = (core if side else 1 - core) * pairs + i
            for j, src in enumerate((x_hbm, q_hbm, v_hbm)):
                pltpu.make_async_copy(src.at[e], in_buf.at[i, side, j], load_sem.at[i]).start()
        return 0

    lax.fori_loop(0, pairs, start_loads, 0)
    t_copy = pltpu.make_async_copy(t_hbm, t_buf, t_sem)
    t_copy.start()

    fixed[0].wait()
    sketch = sketch_ref[...]

    def placed(slot):
        row = lax.broadcasted_iota(jnp.int32, (rc, 128), 0)
        col = lax.broadcasted_iota(jnp.int32, (rc, 128), 1)
        here = jnp.logical_or(col == row + slot * rc, col == row + slot * rc + ranks)
        return mm(sketch, jnp.where(here, 1.0, 0.0).astype(BF16), 0, 0).astype(BF16)

    spread = [placed(slot) for slot in range(4)]
    fixed[1].wait()
    w_buf[0, :, :128] = (mm(red_ref[0], spread[2]) + mm(red_ref[1], spread[3])).astype(BF16)
    fixed[2].wait()
    w_buf[1, :, :128] = mm(exp_ref[0], spread[0], 0, 0).astype(BF16)
    w_buf[2, :, :128] = mm(exp_ref[1], spread[1], 0, 0).astype(BF16)
    arrived(w_buf.at[:, :, 128:], fixed_sem.at[3])
    fixed[6].wait()

    lower, upper_plane = jnp.where(d > 0, 1, 0), jnp.where(d < nd - 1, 1, 0)

    def tell():
        @pl.when(d > 0)
        def _():
            signal(high_sem, d - 1, c)

        @pl.when(d < nd - 1)
        def _():
            signal(low_sem, d + 1, c)

    def hear():
        @pl.when(d > 0)
        def _():
            pl.semaphore_wait(low_sem, 1)

        @pl.when(d < nd - 1)
        def _():
            pl.semaphore_wait(high_sem, 1)

    def project(e, side, wide, i, out):
        row = lax.broadcasted_iota(jnp.int32, (half, 128), 0)
        upper = lax.broadcasted_iota(jnp.int32, (half, 128), 1) >= ranks
        live = jnp.where(upper, row + half, row) < len_ref[e]
        for k in range(half // 128):
            sums = []
            for late in range(2):
                span = pl.ds(late * half + k * 128, 128)
                narrow = None
                for j in range(3):
                    res = mm(in_buf[i, side, j, span], w_buf[j])
                    wide[i, span, j * 128 : (j + 1) * 128] = res[:, 128:].astype(BF16)
                    narrow = res[:, :128] if narrow is None else narrow + res[:, :128]
                sums.append(narrow)
            packed = jnp.where(upper[:128], sums[1], sums[0])
            packed = jnp.where(live[k * 128 : (k + 1) * 128], packed, 0.0).astype(BF16)
            out[i, :, :, k * 128 : (k + 1) * 128] = packed.T.reshape(PARTS, ranks, 128)

    def pair_copy(i):
        return remote(pair_out.at[i], pair_in.at[i], send_sem.at[0], pair_r.at[i], d, partner)

    def wide_copy(i):
        return remote(wide_out.at[i], wide_in.at[i], send_sem.at[1], wide_r.at[i], d, partner)

    def step_copy(i, level, part):
        return remote(
            comb.at[i, level, part],
            step_in.at[i, level, part],
            send_sem.at[2],
            step_r.at[i, level],
            d,
            across((level + part) % levels),
        )

    def feat_copy(b, r):
        to = lax.rem(c + r, n)
        return remote(feat_out.at[b, to], feat_in.at[b, r], send_sem.at[3], feat_r.at[b], d, to)

    def u_copy(b, r, place):
        to = lax.rem(d + r, nd)
        return remote(u_all.at[b, place], u_all.at[b, place], send_sem.at[4], u_r.at[b], to, c)

    def sq_copy(r):
        to = lax.rem(c + r, n)
        return remote(sq_out, sq_in.at[r], send_sem.at[5], sq_r, d, to)

    def home(h):
        return (d * own_targets + h * piece) // out_cols, lax.rem(d * own_targets + h * piece, out_cols) // piece

    def t_copy_out(i, h):
        j, s = home(h)
        return remote(t_out.at[h], t_in.at[s, c], tn_s.at[h], tn_r.at[s], i, j)

    def g_copy(i, h):
        j, s = home(h)
        return remote(g_out.at[i, h], g_in.at[s, c], g_s.at[h], g_r.at[s], i, j)

    def scatter_pieces(make, own_in, own_out):
        for i in range(nd):
            for h in range(halves):
                j, s = home(h)
                here = jnp.logical_and(d == i, c == j)

                @pl.when(jnp.logical_not(here))
                def _():
                    make(i, h).start()

                @pl.when(here)
                def _():
                    own_in[s, c] = own_out(i, h)

    def drain_pieces(like, send):
        for h in range(halves):
            j, _ = home(h)

            @pl.when(c == j)
            def _():
                sent(like(nd - 1), send.at[h])

            @pl.when(c != j)
            def _():
                sent(like(nd), send.at[h])

    def receive_pieces(buf, recv):
        for s in range(slots):
            source = (c * out_cols + s * piece) // own_targets

            @pl.when(d == source)
            def _():
                received(buf.at[s, : n - 1], recv.at[s])

            @pl.when(d != source)
            def _():
                received(buf.at[s], recv.at[s])

    def turn(it, lag):
        return jnp.logical_and(it >= lag, it < pairs + lag)

    def step(it, _):
        @pl.when(it < pairs)
        def _():
            arrived(in_buf.at[it], load_sem.at[it])
            project((1 - core) * pairs + it, 0, wide_out, it, pair_out)
            project(core * pairs + it, 1, wide_own, it, mine)

            @pl.when(it == 0)
            def _():
                pl.semaphore_wait(barrier, 1 + levels + lower + upper_plane)
                if nd > 2:
                    tell()

            pair_copy(it).start()
            wide_copy(it).start()

        @pl.when(turn(it, 1))
        def _():
            i = it - 1
            pair_copy(i).wait_recv()
            for part in range(PARTS):
                comb[i, 0, part] = (mine[i, part].astype(F32) + pair_in[i, part].astype(F32)).astype(BF16)
                step_copy(i, 0, part).start()

        for level in range(1, levels):

            @pl.when(turn(it, 1 + LAG * level))
            def _():
                i = it - (1 + LAG * level)
                received(step_in.at[i, level - 1], step_r.at[i, level - 1])
                for part in range(PARTS):
                    both = comb[i, level - 1, part].astype(F32) + step_in[i, level - 1, part].astype(F32)
                    comb[i, level, part] = both.astype(BF16)
                    step_copy(i, level, part).start()

        @pl.when(turn(it, last_lag))
        def _():
            i = it - last_lag
            wide_copy(i).wait_recv()
            received(step_in.at[i, levels - 1], step_r.at[i, levels - 1])
            whole = []
            for part in range(PARTS):
                both = comb[i, levels - 1, part].astype(F32) + step_in[i, levels - 1, part].astype(F32)
                whole.append(both.astype(BF16))
            g = jnp.concatenate(whole, axis=1)
            left = mm(g, wide_own[i, :, :256]) + mm(g, wide_in[i, :, :256])
            right = mm(g[3 * rc :], wide_own[i, :, 256:]) + mm(g[3 * rc :], wide_in[i, :, 256:])
            b, place = i // per, lax.rem(i, per)
            found[place, : 2 * rc] = left[: 2 * rc, :128]
            found[place, 2 * rc : 3 * rc] = left[2 * rc : 3 * rc, 128:]
            found[place, 3 * rc :] = right

            @pl.when(place == per - 1)
            def _():
                for q in range(n):
                    feat_out[b, q] = jnp.concatenate(
                        [found[p, q * rows : (q + 1) * rows] for p in range(per)], axis=0
                    ).astype(BF16)
                for r in range(1, n):
                    feat_copy(b, r).start()

        if nd > 2:

            @pl.when(jnp.logical_and(lax.rem(it, 2) == 0, jnp.logical_and(it >= 2, it <= 2 * (nd - 2))))
            def _():
                hear()

                @pl.when(it < 2 * (nd - 2))
                def _():
                    tell()

        @pl.when(it == pairs)
        def _():
            t_copy.wait()
            t = t_buf[...].astype(F32)
            norm = jnp.broadcast_to(jnp.sum(t * t, axis=1, keepdims=True), (own_targets, 128)).T
            for h in range(halves):
                t_out[h] = norm[:8, h * piece : (h + 1) * piece]

        return 0

    lax.fori_loop(0, max(pairs + last_lag, 2 * (nd - 2) + 1), step, 0)

    arrived(m_ref, fixed_sem.at[5])
    m1 = jnp.concatenate([m_ref[0, c]] * per, axis=0)
    m2 = jnp.concatenate([m_ref[1, c]] * per, axis=0)

    def keep(b, i, k, u):
        u = u.astype(F32)
        for p in range(per):
            u_f32[i * examples + k * pairs + b * per + p] = u[p * rows : (p + 1) * rows]

    for b in range(batches):
        sums = [feat_out[b, c].astype(F32), None]
        received(feat_in.at[b, 1:], feat_r.at[b])
        for r in range(1, n):
            f = feat_in[b, r].astype(F32)
            sums[r % 2] = f if sums[r % 2] is None else sums[r % 2] + f
        for f, k in ((sums[0], core), (sums[1], 1 - core)):
            new = (0.9 * m1 + 0.1 * f) / (jnp.sqrt(0.999 * m2 + 0.001 * f * f) + 1e-08)
            u = new.astype(BF16)
            u_all[b, d, k] = u
            keep(b, d, k, u)
        for r in range(1, nd):
            u_copy(b, r, d).start()

    squares = None
    for r in range(rows):
        u = u_f32[pl.ds(d * examples, examples), r, :]
        squares = u * u if squares is None else squares + u * u
    sq_out[...] = squares
    for r in range(1, n):
        sq_copy(r).start()

    for b in range(batches):
        received(u_all.at[b, : nd - 1], u_r.at[b])
        for r in range(1, nd):
            source = lax.rem(d + nd - r, nd)
            for k in range(2):
                keep(b, source, k, u_all[b, source, k])
        if b == 0:
            scatter_pieces(t_copy_out, t_in, lambda i, h: t_out[h])

    u_rows = jnp.concatenate([u_f32[:, r, :].astype(BF16) for r in range(rows)], axis=1)
    dots = mm(u_rows, t_buf[...], 1, 1).astype(BF16)
    for i in range(nd):
        for h in range(halves):
            g_out[i, h] = dots[i * examples : (i + 1) * examples, h * piece : (h + 1) * piece]
    scatter_pieces(g_copy, g_in, lambda i, h: g_out[i, h])

    received(sq_in.at[1:], sq_r)
    for r in range(1, n):
        squares = squares + sq_in[r]
    row_scale = lax.rsqrt(jnp.sum(squares, axis=1, keepdims=True) + 1e-06) * math.sqrt(ranks * 128)
    receive_pieces(t_in, tn_r)
    column_scale = []
    for s in range(slots):
        norm = t_in[s, 0]
        for cc in range(1, n):
            norm = norm + t_in[s, cc]
        column_scale.append(lax.rsqrt(norm[:1] + 1e-06))
    receive_pieces(g_in, g_r)
    for s in range(slots):
        acc = g_in[s, 0].astype(F32)
        for cc in range(1, n):
            acc = acc + g_in[s, cc].astype(F32)
        out_ref[:, s * piece : (s + 1) * piece] = acc * row_scale * column_scale[s]

    sent(pair_out, send_sem.at[0])
    sent(wide_out, send_sem.at[1])
    sent(comb, send_sem.at[2])
    sent(feat_out.at[:, 1:], send_sem.at[3])
    sent(u_all.at[:, 1:], send_sem.at[4])
    sent(sq_in.at[1:], send_sem.at[5])
    drain_pieces(lambda count: t_in.at[0, :count], tn_s)
    drain_pieces(lambda count: g_out.at[:count, 0], g_s)


def body(nd, n, x, q, v, lengths, reducing, expanding, width, sketch, m1, m2, targets):
    examples, seq, depth = x.shape
    ranks = 4 * sketch.shape[1]
    pairs, chips, rows = examples // 2, n // 2, ranks // n
    levels = chips.bit_length() - 1
    half = seq // 2
    per = max(1, 16 // rows)
    batches = pairs // per
    own_targets = targets.shape[0]
    out_cols = own_targets * nd // n
    piece = min(own_targets, out_cols)
    halves, slots = own_targets // piece, out_cols // piece
    dma = pltpu.SemaphoreType.DMA
    anywhere = pl.BlockSpec(memory_space=pl.ANY)
    vmem = pl.BlockSpec(memory_space=pltpu.VMEM)
    return pl.pallas_call(
        functools.partial(kernel, nd, n),
        out_shape=jax.ShapeDtypeStruct((examples, out_cols), F32),
        in_specs=[anywhere] * 11,
        out_specs=vmem,
        scratch_shapes=[
            pltpu.VMEM((pairs, 2, 3, seq, depth), BF16),
            pltpu.VMEM(targets.shape, BF16),
            pltpu.SMEM((examples,), jnp.int32),
            pltpu.VMEM(sketch.shape[::-1], BF16),
            pltpu.VMEM((2, n, rows, 128), F32),
            pltpu.VMEM(reducing.shape, BF16),
            pltpu.VMEM(expanding.shape, BF16),
            pltpu.VMEM((3, depth, 256), BF16),
            pltpu.VMEM((pairs, seq, 384), BF16),
            pltpu.VMEM((pairs, seq, 384), BF16),
            pltpu.VMEM((pairs, seq, 384), BF16),
            pltpu.VMEM((pairs, PARTS, ranks, half), BF16),
            pltpu.VMEM((pairs, PARTS, ranks, half), BF16),
            pltpu.VMEM((pairs, PARTS, ranks, half), BF16),
            pltpu.VMEM((pairs, levels, PARTS, ranks, half), BF16),
            pltpu.VMEM((pairs, levels, PARTS, ranks, half), BF16),
            pltpu.VMEM((per, ranks, 128), F32),
            pltpu.VMEM((batches, n, per * rows, 128), BF16),
            pltpu.VMEM((batches, n, per * rows, 128), BF16),
            pltpu.VMEM((batches, nd, 2, per * rows, 128), BF16),
            pltpu.VMEM((nd * examples, rows, 128), F32),
            pltpu.VMEM((examples, 128), F32),
            pltpu.VMEM((n, examples, 128), F32),
            pltpu.VMEM((halves, 8, piece), F32),
            pltpu.VMEM((slots, n, 8, piece), F32),
            pltpu.VMEM((nd, halves, examples, piece), BF16),
            pltpu.VMEM((slots, n, examples, piece), BF16),
            dma((pairs,)),
            dma,
            dma((6,)),
            dma((6,)),
            dma((pairs,)),
            dma((pairs,)),
            dma((pairs, levels)),
            dma((batches,)),
            dma((batches,)),
            dma,
            dma((halves,)),
            dma((slots,)),
            dma((halves,)),
            dma((slots,)),
            pltpu.SemaphoreType.REGULAR,
            pltpu.SemaphoreType.REGULAR,
        ],
        compiler_params=pltpu.CompilerParams(
            collective_id=0, has_side_effects=True, vmem_limit_bytes=56 * 1024 * 1024
        ),
    )(
        x,
        q,
        v,
        lengths,
        reducing,
        expanding,
        width,
        sketch.T,
        m1.reshape(n, rows, 128),
        m2.reshape(n, rows, 128),
        targets,
    )


def solution(mesh):
    placed = (
        P("dp", None, "tp"),
        P("dp", None, "tp"),
        P("dp", None, "tp"),
        P("dp"),
        P(None, "tp", None),
        P(None, None, "tp"),
        P(None, "tp", None),
        P(),
        P(),
        P(),
        P("dp", "tp"),
    )
    names = mesh.axis_names
    order = (mesh.shape["dp"], mesh.shape["tp"])
    run = functools.partial(body, *order)
    assert set(names) == {"dp", "tp"}
    return jax.shard_map(run, mesh=mesh, in_specs=placed, out_specs=P("dp", "tp"), check_vma=False)
```

```python
import functools
import math

import jax
import jax.numpy as jnp
from jax import lax
from jax.experimental import pallas as pl
from jax.experimental.pallas import tpu as pltpu
from jax.sharding import PartitionSpec as P

MESH = pl.DeviceIdType.MESH
F32 = jnp.float32
BF16 = jnp.bfloat16
PARTS = 2
LAG = 3


def mm(a, b, ca=1, cb=0):
    return lax.dot_general(a, b, (((ca,), (cb,)), ((), ())), preferred_element_type=F32)


def kernel(
    nd,
    n,
    x_hbm,
    q_hbm,
    v_hbm,
    len_hbm,
    red_hbm,
    exp_hbm,
    width_hbm,
    sketch_hbm,
    m1_hbm,
    m2_hbm,
    t_hbm,
    out_ref,
    in_buf,
    t_all,
    t_turned,
    norms,
    len_ref,
    sketch_ref,
    m_ref,
    red_ref,
    exp_ref,
    w_buf,
    wide_out,
    wide_in,
    wide_own,
    pair_out,
    pair_in,
    mine,
    comb,
    step_in,
    found,
    feat_out,
    feat_in,
    u_all,
    u_f32,
    sq_out,
    sq_in,
    t_out,
    t_in,
    g_out,
    g_in,
    load_sem,
    t_sem,
    fixed_sem,
    send_sem,
    pair_r,
    wide_r,
    step_r,
    feat_r,
    u_r,
    sq_r,
    tn_s,
    tn_r,
    g_s,
    g_r,
    mate_s,
    mate_r,
    low_sem,
    high_sem,
):
    d = lax.axis_index("dp")
    c = lax.axis_index("tp")
    chips = n // 2
    levels = chips.bit_length() - 1
    chip, core = c // 2, lax.rem(c, 2)
    partner = chip * 2 + 1 - core
    pairs, _, _, seq, depth = in_buf.shape
    examples = pairs * 2
    rc = sketch_ref.shape[0]
    ranks = 4 * rc
    half = seq // 2
    rows = ranks // n
    batches, _, tile, _ = feat_out.shape
    per = tile // rows
    parity, mate = lax.rem(d, 2), d + 1 - 2 * lax.rem(d, 2)
    own_targets = t_all.shape[1]
    group, groups, shared = d // 2, nd // 2, 2 * own_targets
    out_cols = out_ref.shape[1]
    piece = min(shared, out_cols)
    halves = shared // piece
    slots = out_cols // piece
    far = nd - 3
    last_lag = 1 + LAG * levels

    def remote(src, dst, send, recv, dd, cc):
        return pltpu.make_async_remote_copy(
            src_ref=src, dst_ref=dst, send_sem=send, recv_sem=recv, device_id={"dp": dd, "tp": cc}, device_id_type=MESH
        )

    def arrived(block, sem):
        pltpu.make_async_copy(block, block, sem).wait()

    def received(block, sem):
        remote(block, block, sem, sem, d, partner).wait_recv()

    def sent(block, sem):
        remote(block, block, sem, sem, d, partner).wait_send()

    def signal(sem, dd, cc):
        pl.semaphore_signal(sem, inc=1, device_id={"dp": dd, "tp": cc}, device_id_type=MESH)

    def across(bit):
        m = 1 << bit
        return (chip + m * (1 - 2 * lax.rem(chip // m, 2))) * 2 + core

    barrier = pltpu.get_barrier_semaphore()
    signal(barrier, d, partner)
    for bit in range(levels):
        signal(barrier, d, across(bit))

    @pl.when(d > 0)
    def _():
        signal(barrier, d - 1, c)

    @pl.when(d < nd - 1)
    def _():
        signal(barrier, d + 1, c)

    fixed = [
        pltpu.make_async_copy(src, dst, fixed_sem.at[j])
        for src, dst, j in [(sketch_hbm, sketch_ref, 0), (red_hbm, red_ref, 1), (exp_hbm, exp_ref, 2)]
        + [(width_hbm.at[min(j, 1)], w_buf.at[j, :, 128:], 3) for j in range(3)]
        + [(len_hbm, len_ref, 4), (m1_hbm, m_ref.at[0], 5), (m2_hbm, m_ref.at[1], 5)]
    ]
    for copy in fixed:
        copy.start()

    def start_loads(i, _):
        for side in range(2):
            e = (core if side else 1 - core) * pairs + i
            for j, src in enumerate((x_hbm, q_hbm, v_hbm)):
                pltpu.make_async_copy(src.at[e], in_buf.at[i, side, j], load_sem.at[i]).start()
        return 0

    lax.fori_loop(0, pairs, start_loads, 0)
    t_copy = pltpu.make_async_copy(t_hbm, t_all.at[parity], t_sem)
    t_copy.start()

    fixed[0].wait()
    sketch = sketch_ref[...]

    def placed(slot):
        row = lax.broadcasted_iota(jnp.int32, (rc, 128), 0)
        col = lax.broadcasted_iota(jnp.int32, (rc, 128), 1)
        here = jnp.logical_or(col == row + slot * rc, col == row + slot * rc + ranks)
        return mm(sketch, jnp.where(here, 1.0, 0.0).astype(BF16), 0, 0).astype(BF16)

    spread = [placed(slot) for slot in range(4)]
    fixed[1].wait()
    w_buf[0, :, :128] = (mm(red_ref[0], spread[2]) + mm(red_ref[1], spread[3])).astype(BF16)
    fixed[2].wait()
    w_buf[1, :, :128] = mm(exp_ref[0], spread[0], 0, 0).astype(BF16)
    w_buf[2, :, :128] = mm(exp_ref[1], spread[1], 0, 0).astype(BF16)
    arrived(w_buf.at[:, :, 128:], fixed_sem.at[3])
    fixed[6].wait()

    lower, upper_plane = jnp.where(d > 0, 1, 0), jnp.where(d < nd - 1, 1, 0)

    def tell():
        @pl.when(d > 0)
        def _():
            signal(high_sem, d - 1, c)

        @pl.when(d < nd - 1)
        def _():
            signal(low_sem, d + 1, c)

    def hear():
        @pl.when(d > 0)
        def _():
            pl.semaphore_wait(low_sem, 1)

        @pl.when(d < nd - 1)
        def _():
            pl.semaphore_wait(high_sem, 1)

    def project(e, side, wide, i, out):
        row = lax.broadcasted_iota(jnp.int32, (half, 128), 0)
        upper = lax.broadcasted_iota(jnp.int32, (half, 128), 1) >= ranks
        live = jnp.where(upper, row + half, row) < len_ref[e]
        for k in range(half // 128):
            sums = []
            for late in range(2):
                span = pl.ds(late * half + k * 128, 128)
                narrow = None
                for j in range(3):
                    res = mm(in_buf[i, side, j, span], w_buf[j])
                    wide[i, span, j * 128 : (j + 1) * 128] = res[:, 128:].astype(BF16)
                    narrow = res[:, :128] if narrow is None else narrow + res[:, :128]
                sums.append(narrow)
            packed = jnp.where(upper[:128], sums[1], sums[0])
            packed = jnp.where(live[k * 128 : (k + 1) * 128], packed, 0.0).astype(BF16)
            out[i, :, :, k * 128 : (k + 1) * 128] = packed.T.reshape(PARTS, ranks, 128)

    def pair_copy(i):
        return remote(pair_out.at[i], pair_in.at[i], send_sem.at[0], pair_r.at[i], d, partner)

    def wide_copy(i):
        return remote(wide_out.at[i], wide_in.at[i], send_sem.at[1], wide_r.at[i], d, partner)

    def step_copy(i, level, part):
        return remote(
            comb.at[i, level, part],
            step_in.at[i, level, part],
            send_sem.at[2],
            step_r.at[i, level],
            d,
            across((level + part) % levels),
        )

    def feat_copy(b, r):
        to = lax.rem(c + r, n)
        return remote(feat_out.at[b, to], feat_in.at[b, r], send_sem.at[3], feat_r.at[b], d, to)

    def u_copy(b, r, place):
        to = lax.rem(group + r, groups) * 2 + parity
        return remote(u_all.at[b, place], u_all.at[b, place], send_sem.at[4], u_r.at[b], to, c)

    def sq_copy(r):
        to = lax.rem(c + r, n)
        return remote(sq_out, sq_in.at[r], send_sem.at[5], sq_r, d, to)

    def home(h):
        first = group * shared + h * piece
        return first // out_cols, lax.rem(first, out_cols) // piece

    def t_copy_out(k, h):
        j, s = home(h)
        return remote(t_out.at[h], t_in.at[s, c], tn_s.at[h], tn_r.at[s], k * 2 + parity, j)

    def g_copy(k, h):
        j, s = home(h)
        return remote(g_out.at[k, h], g_in.at[s, c], g_s.at[h], g_r.at[s], k * 2 + parity, j)

    def scatter_pieces(make, own_in, own_out):
        for k in range(groups):
            for h in range(halves):
                j, s = home(h)
                here = jnp.logical_and(group == k, c == j)

                @pl.when(jnp.logical_not(here))
                def _():
                    make(k, h).start()

                @pl.when(here)
                def _():
                    own_in[s, c] = own_out(k, h)

    def drain_pieces(like, send):
        for h in range(halves):
            j, _ = home(h)

            @pl.when(c == j)
            def _():
                sent(like(groups - 1), send.at[h])

            @pl.when(c != j)
            def _():
                sent(like(groups), send.at[h])

    def receive_pieces(buf, recv):
        for s in range(slots):
            source = (c * out_cols + s * piece) // shared

            @pl.when(group == source)
            def _():
                received(buf.at[s, : n - 1], recv.at[s])

            @pl.when(group != source)
            def _():
                received(buf.at[s], recv.at[s])

    def turn_targets(side):
        t = t_all[side].T
        t_turned[side] = t
        t = t.astype(F32)
        norms[side] = jnp.broadcast_to(jnp.sum(t * t, axis=0, keepdims=True), (8, own_targets))

    def turn(it, lag):
        return jnp.logical_and(it >= lag, it < pairs + lag)

    def step(it, _):
        @pl.when(it < pairs)
        def _():
            arrived(in_buf.at[it], load_sem.at[it])
            project((1 - core) * pairs + it, 0, wide_out, it, pair_out)
            project(core * pairs + it, 1, wide_own, it, mine)

            @pl.when(it == 0)
            def _():
                pl.semaphore_wait(barrier, 1 + levels + lower + upper_plane)
                remote(t_hbm, t_all.at[parity], mate_s, mate_r, mate, c).start()
                if far > 0:
                    tell()

            pair_copy(it).start()
            wide_copy(it).start()

        @pl.when(turn(it, 1))
        def _():
            i = it - 1
            pair_copy(i).wait_recv()
            for part in range(PARTS):
                comb[i, 0, part] = (mine[i, part].astype(F32) + pair_in[i, part].astype(F32)).astype(BF16)
                step_copy(i, 0, part).start()

        for level in range(1, levels):

            @pl.when(turn(it, 1 + LAG * level))
            def _():
                i = it - (1 + LAG * level)
                received(step_in.at[i, level - 1], step_r.at[i, level - 1])
                for part in range(PARTS):
                    both = comb[i, level - 1, part].astype(F32) + step_in[i, level - 1, part].astype(F32)
                    comb[i, level, part] = both.astype(BF16)
                    step_copy(i, level, part).start()

        @pl.when(turn(it, last_lag))
        def _():
            i = it - last_lag
            wide_copy(i).wait_recv()
            received(step_in.at[i, levels - 1], step_r.at[i, levels - 1])
            whole = []
            for part in range(PARTS):
                both = comb[i, levels - 1, part].astype(F32) + step_in[i, levels - 1, part].astype(F32)
                whole.append(both.astype(BF16))
            g = jnp.concatenate(whole, axis=1)
            left = mm(g, wide_own[i, :, :256]) + mm(g, wide_in[i, :, :256])
            right = mm(g[3 * rc :], wide_own[i, :, 256:]) + mm(g[3 * rc :], wide_in[i, :, 256:])
            b, place = i // per, lax.rem(i, per)
            found[place, : 2 * rc] = left[: 2 * rc, :128]
            found[place, 2 * rc : 3 * rc] = left[2 * rc : 3 * rc, 128:]
            found[place, 3 * rc :] = right

            @pl.when(place == per - 1)
            def _():
                for q in range(n):
                    feat_out[b, q] = jnp.concatenate(
                        [found[p, q * rows : (q + 1) * rows] for p in range(per)], axis=0
                    ).astype(BF16)
                for r in range(1, n):
                    feat_copy(b, r).start()

        if far > 0:

            @pl.when(jnp.logical_and(lax.rem(it, 2) == 0, jnp.logical_and(it >= 2, it <= 2 * far)))
            def _():
                hear()

                @pl.when(it < 2 * far)
                def _():
                    tell()

        @pl.when(it == pairs)
        def _():
            t_copy.wait()
            turn_targets(parity)

        @pl.when(it == pairs + 2)
        def _():
            received(t_all.at[1 - parity], mate_r)
            turn_targets(1 - parity)

        return 0

    lax.fori_loop(0, max(pairs + last_lag, 2 * far + 1), step, 0)

    arrived(m_ref, fixed_sem.at[5])
    m1 = jnp.concatenate([m_ref[0, c]] * per, axis=0)
    m2 = jnp.concatenate([m_ref[1, c]] * per, axis=0)

    norm = jnp.concatenate([norms[0], norms[1]], axis=1)
    for h in range(halves):
        t_out[h] = norm[:, h * piece : (h + 1) * piece]

    def keep(b, i, k, u):
        u = u.astype(F32)
        for p in range(per):
            u_f32[i * examples + k * pairs + b * per + p] = u[p * rows : (p + 1) * rows]

    for b in range(batches):
        sums = [feat_out[b, c].astype(F32), None]
        received(feat_in.at[b, 1:], feat_r.at[b])
        for r in range(1, n):
            f = feat_in[b, r].astype(F32)
            sums[r % 2] = f if sums[r % 2] is None else sums[r % 2] + f
        for f, k in ((sums[0], core), (sums[1], 1 - core)):
            new = (0.9 * m1 + 0.1 * f) / (jnp.sqrt(0.999 * m2 + 0.001 * f * f) + 1e-08)
            u = new.astype(BF16)
            u_all[b, group, k] = u
            keep(b, group, k, u)
        for r in range(1, groups):
            u_copy(b, r, group).start()

    squares = None
    for r in range(rows):
        u = u_f32[pl.ds(group * examples, examples), r, :]
        squares = u * u if squares is None else squares + u * u
    sq_out[...] = squares
    for r in range(1, n):
        sq_copy(r).start()

    for b in range(batches):
        received(u_all.at[b, : groups - 1], u_r.at[b])
        for r in range(1, groups):
            source = lax.rem(group + groups - r, groups)
            for k in range(2):
                keep(b, source, k, u_all[b, source, k])
        if b == 0:
            scatter_pieces(t_copy_out, t_in, lambda k, h: t_out[h])

    u_rows = jnp.concatenate([u_f32[:, r, :].astype(BF16) for r in range(rows)], axis=1)
    dots = jnp.concatenate([mm(u_rows, t_turned[side]) for side in range(2)], axis=1).astype(BF16)
    for k in range(groups):
        for h in range(halves):
            g_out[k, h] = dots[k * examples : (k + 1) * examples, h * piece : (h + 1) * piece]
    scatter_pieces(g_copy, g_in, lambda k, h: g_out[k, h])

    received(sq_in.at[1:], sq_r)
    for r in range(1, n):
        squares = squares + sq_in[r]
    row_scale = lax.rsqrt(jnp.sum(squares, axis=1, keepdims=True) + 1e-06) * math.sqrt(ranks * 128)
    receive_pieces(t_in, tn_r)
    column_scale = []
    for s in range(slots):
        norm = t_in[s, 0]
        for cc in range(1, n):
            norm = norm + t_in[s, cc]
        column_scale.append(lax.rsqrt(norm[:1] + 1e-06))
    receive_pieces(g_in, g_r)
    for s in range(slots):
        acc = g_in[s, 0].astype(F32)
        for cc in range(1, n):
            acc = acc + g_in[s, cc].astype(F32)
        out_ref[:, s * piece : (s + 1) * piece] = acc * row_scale * column_scale[s]

    sent(pair_out, send_sem.at[0])
    sent(wide_out, send_sem.at[1])
    sent(comb, send_sem.at[2])
    sent(feat_out.at[:, 1:], send_sem.at[3])
    sent(u_all.at[:, 1:], send_sem.at[4])
    sent(t_all.at[parity], mate_s)
    sent(sq_in.at[1:], send_sem.at[5])
    drain_pieces(lambda count: t_in.at[0, :count], tn_s)
    drain_pieces(lambda count: g_out.at[:count, 0], g_s)


def body(nd, n, x, q, v, lengths, reducing, expanding, width, sketch, m1, m2, targets):
    examples, seq, depth = x.shape
    ranks = 4 * sketch.shape[1]
    pairs, chips, rows = examples // 2, n // 2, ranks // n
    levels = chips.bit_length() - 1
    half = seq // 2
    per = max(1, 16 // rows)
    batches = pairs // per
    own_targets = targets.shape[0]
    out_cols = own_targets * nd // n
    shared, groups = 2 * own_targets, nd // 2
    piece = min(shared, out_cols)
    halves, slots = shared // piece, out_cols // piece
    dma = pltpu.SemaphoreType.DMA
    anywhere = pl.BlockSpec(memory_space=pl.ANY)
    vmem = pl.BlockSpec(memory_space=pltpu.VMEM)
    return pl.pallas_call(
        functools.partial(kernel, nd, n),
        out_shape=pltpu.VMEM((examples, out_cols), F32),
        in_specs=[anywhere] * 11,
        out_specs=vmem,
        scratch_shapes=[
            pltpu.VMEM((pairs, 2, 3, seq, depth), BF16),
            pltpu.VMEM((2, *targets.shape), BF16),
            pltpu.VMEM((2, *targets.shape[::-1]), BF16),
            pltpu.VMEM((2, 8, own_targets), F32),
            pltpu.SMEM((examples,), jnp.int32),
            pltpu.VMEM(sketch.shape[::-1], BF16),
            pltpu.VMEM((2, n, rows, 128), F32),
            pltpu.VMEM(reducing.shape, BF16),
            pltpu.VMEM(expanding.shape, BF16),
            pltpu.VMEM((3, depth, 256), BF16),
            pltpu.VMEM((pairs, seq, 384), BF16),
            pltpu.VMEM((pairs, seq, 384), BF16),
            pltpu.VMEM((pairs, seq, 384), BF16),
            pltpu.VMEM((pairs, PARTS, ranks, half), BF16),
            pltpu.VMEM((pairs, PARTS, ranks, half), BF16),
            pltpu.VMEM((pairs, PARTS, ranks, half), BF16),
            pltpu.VMEM((pairs, levels, PARTS, ranks, half), BF16),
            pltpu.VMEM((pairs, levels, PARTS, ranks, half), BF16),
            pltpu.VMEM((per, ranks, 128), F32),
            pltpu.VMEM((batches, n, per * rows, 128), BF16),
            pltpu.VMEM((batches, n, per * rows, 128), BF16),
            pltpu.VMEM((batches, groups, 2, per * rows, 128), BF16),
            pltpu.VMEM((groups * examples, rows, 128), F32),
            pltpu.VMEM((examples, 128), F32),
            pltpu.VMEM((n, examples, 128), F32),
            pltpu.VMEM((halves, 8, piece), F32),
            pltpu.VMEM((slots, n, 8, piece), F32),
            pltpu.VMEM((groups, halves, examples, piece), BF16),
            pltpu.VMEM((slots, n, examples, piece), BF16),
            dma((pairs,)),
            dma,
            dma((6,)),
            dma((6,)),
            dma((pairs,)),
            dma((pairs,)),
            dma((pairs, levels)),
            dma((batches,)),
            dma((batches,)),
            dma,
            dma((halves,)),
            dma((slots,)),
            dma((halves,)),
            dma((slots,)),
            dma,
            dma,
            pltpu.SemaphoreType.REGULAR,
            pltpu.SemaphoreType.REGULAR,
        ],
        compiler_params=pltpu.CompilerParams(
            collective_id=0, has_side_effects=True, vmem_limit_bytes=56 * 1024 * 1024
        ),
    )(
        x,
        q,
        v,
        lengths,
        reducing,
        expanding,
        width,
        sketch.T,
        m1.reshape(n, rows, 128),
        m2.reshape(n, rows, 128),
        targets,
    )


def solution(mesh):
    placed = (
        P("dp", None, "tp"),
        P("dp", None, "tp"),
        P("dp", None, "tp"),
        P("dp"),
        P(None, "tp", None),
        P(None, None, "tp"),
        P(None, "tp", None),
        P(),
        P(),
        P(),
        P("dp", "tp"),
    )
    names = mesh.axis_names
    order = (mesh.shape["dp"], mesh.shape["tp"])
    run = functools.partial(body, *order)
    assert set(names) == {"dp", "tp"}
    return jax.shard_map(run, mesh=mesh, in_specs=placed, out_specs=P("dp", "tp"), check_vma=False)
```

```python
import functools
import math

import jax
import jax.numpy as jnp
from jax import lax
from jax.experimental import pallas as pl
from jax.experimental.pallas import tpu as pltpu
from jax.sharding import PartitionSpec as P

MESH = pl.DeviceIdType.MESH
F32 = jnp.float32
BF16 = jnp.bfloat16
PARTS = 2
LAG = 3


def mm(a, b, ca=1, cb=0):
    return lax.dot_general(a, b, (((ca,), (cb,)), ((), ())), preferred_element_type=F32)


def kernel(
    nd,
    n,
    x_hbm,
    q_hbm,
    v_hbm,
    len_hbm,
    red_hbm,
    exp_hbm,
    width_hbm,
    sketch_hbm,
    m1_hbm,
    m2_hbm,
    t_hbm,
    out_ref,
    in_buf,
    t_all,
    t_turned,
    norms,
    len_ref,
    sketch_ref,
    m_ref,
    red_ref,
    exp_ref,
    w_buf,
    wide_out,
    wide_in,
    wide_own,
    pair_out,
    pair_in,
    mine,
    comb,
    step_in,
    found,
    feat_out,
    feat_in,
    u_all,
    u_f32,
    sq_out,
    sq_in,
    t_out,
    t_in,
    g_out,
    g_in,
    load_sem,
    t_sem,
    fixed_sem,
    send_sem,
    pair_r,
    wide_r,
    step_r,
    feat_r,
    u_r,
    sq_r,
    tn_s,
    tn_r,
    g_s,
    g_r,
    mate_s,
    mate_r,
    low_sem,
    high_sem,
):
    d = lax.axis_index("dp")
    c = lax.axis_index("tp")
    chips = n // 2
    levels = chips.bit_length() - 1
    chip, core = c // 2, lax.rem(c, 2)
    partner = chip * 2 + 1 - core
    pairs, _, _, seq, depth = in_buf.shape
    examples = pairs * 2
    rc = sketch_ref.shape[0]
    ranks = 4 * rc
    half = seq // 2
    rows = ranks // n
    batches, _, tile, _ = feat_out.shape
    per = tile // rows
    parity, mate = lax.rem(d, 2), d + 1 - 2 * lax.rem(d, 2)
    own_targets = t_all.shape[1]
    group, groups, shared = d // 2, nd // 2, 2 * own_targets
    out_cols = out_ref.shape[1]
    piece = min(shared, out_cols)
    halves = shared // piece
    slots = out_cols // piece
    far = nd - 3
    last_lag = 1 + LAG * levels

    def remote(src, dst, send, recv, dd, cc):
        return pltpu.make_async_remote_copy(
            src_ref=src, dst_ref=dst, send_sem=send, recv_sem=recv, device_id={"dp": dd, "tp": cc}, device_id_type=MESH
        )

    def arrived(block, sem):
        pltpu.make_async_copy(block, block, sem).wait()

    def received(block, sem):
        remote(block, block, sem, sem, d, partner).wait_recv()

    def sent(block, sem):
        remote(block, block, sem, sem, d, partner).wait_send()

    def signal(sem, dd, cc):
        pl.semaphore_signal(sem, inc=1, device_id={"dp": dd, "tp": cc}, device_id_type=MESH)

    def across(bit):
        m = 1 << bit
        return (chip + m * (1 - 2 * lax.rem(chip // m, 2))) * 2 + core

    barrier = pltpu.get_barrier_semaphore()
    signal(barrier, d, partner)
    for bit in range(levels):
        signal(barrier, d, across(bit))

    @pl.when(d > 0)
    def _():
        signal(barrier, d - 1, c)

    @pl.when(d < nd - 1)
    def _():
        signal(barrier, d + 1, c)

    fixed = [
        pltpu.make_async_copy(src, dst, fixed_sem.at[j])
        for src, dst, j in [(sketch_hbm, sketch_ref, 0), (red_hbm, red_ref, 1), (exp_hbm, exp_ref, 2)]
        + [(width_hbm.at[min(j, 1)], w_buf.at[j, :, 128:], 3) for j in range(3)]
        + [(len_hbm, len_ref, 4), (m1_hbm, m_ref.at[0], 5), (m2_hbm, m_ref.at[1], 5)]
    ]
    for copy in fixed:
        copy.start()

    def start_loads(i, _):
        for side in range(2):
            e = (core if side else 1 - core) * pairs + i
            for j, src in enumerate((x_hbm, q_hbm, v_hbm)):
                pltpu.make_async_copy(src.at[e], in_buf.at[i, side, j], load_sem.at[i]).start()
        return 0

    t_copy = pltpu.make_async_copy(t_hbm, t_all.at[parity], t_sem)
    t_copy.start()
    lax.fori_loop(0, pairs, start_loads, 0)

    fixed[0].wait()
    sketch = sketch_ref[...]

    def placed(slot):
        row = lax.broadcasted_iota(jnp.int32, (rc, 128), 0)
        col = lax.broadcasted_iota(jnp.int32, (rc, 128), 1)
        here = jnp.logical_or(col == row + slot * rc, col == row + slot * rc + ranks)
        return mm(sketch, jnp.where(here, 1.0, 0.0).astype(BF16), 0, 0).astype(BF16)

    spread = [placed(slot) for slot in range(4)]
    fixed[1].wait()
    w_buf[0, :, :128] = (mm(red_ref[0], spread[2]) + mm(red_ref[1], spread[3])).astype(BF16)
    fixed[2].wait()
    w_buf[1, :, :128] = mm(exp_ref[0], spread[0], 0, 0).astype(BF16)
    w_buf[2, :, :128] = mm(exp_ref[1], spread[1], 0, 0).astype(BF16)
    arrived(w_buf.at[:, :, 128:], fixed_sem.at[3])
    fixed[6].wait()

    lower, upper_plane = jnp.where(d > 0, 1, 0), jnp.where(d < nd - 1, 1, 0)

    def tell():
        @pl.when(d > 0)
        def _():
            signal(high_sem, d - 1, c)

        @pl.when(d < nd - 1)
        def _():
            signal(low_sem, d + 1, c)

    def hear():
        @pl.when(d > 0)
        def _():
            pl.semaphore_wait(low_sem, 1)

        @pl.when(d < nd - 1)
        def _():
            pl.semaphore_wait(high_sem, 1)

    def project(e, side, wide, i, out):
        row = lax.broadcasted_iota(jnp.int32, (half, 128), 0)
        upper = lax.broadcasted_iota(jnp.int32, (half, 128), 1) >= ranks
        live = jnp.where(upper, row + half, row) < len_ref[e]
        for k in range(half // 128):
            sums = []
            for late in range(2):
                span = pl.ds(late * half + k * 128, 128)
                narrow = None
                for j in range(3):
                    res = mm(in_buf[i, side, j, span], w_buf[j])
                    wide[i, span, j * 128 : (j + 1) * 128] = res[:, 128:].astype(BF16)
                    narrow = res[:, :128] if narrow is None else narrow + res[:, :128]
                sums.append(narrow)
            packed = jnp.where(upper[:128], sums[1], sums[0])
            packed = jnp.where(live[k * 128 : (k + 1) * 128], packed, 0.0).astype(BF16)
            out[i, :, :, k * 128 : (k + 1) * 128] = packed.T.reshape(PARTS, ranks, 128)

    def pair_copy(i):
        return remote(pair_out.at[i], pair_in.at[i], send_sem.at[0], pair_r.at[i], d, partner)

    def wide_copy(i):
        return remote(wide_out.at[i], wide_in.at[i], send_sem.at[1], wide_r.at[i], d, partner)

    def step_copy(i, level, part):
        return remote(
            comb.at[i, level, part],
            step_in.at[i, level, part],
            send_sem.at[2],
            step_r.at[i, level],
            d,
            across((level + part) % levels),
        )

    def feat_copy(b, r):
        to = lax.rem(c + r, n)
        return remote(feat_out.at[b, to], feat_in.at[b, r], send_sem.at[3], feat_r.at[b], d, to)

    def u_copy(b, r, place):
        to = lax.rem(group + r, groups) * 2 + parity
        return remote(u_all.at[b, place], u_all.at[b, place], send_sem.at[4], u_r.at[b], to, c)

    def sq_copy(r):
        to = lax.rem(c + r, n)
        return remote(sq_out, sq_in.at[r], send_sem.at[5], sq_r, d, to)

    def home(h):
        first = group * shared + h * piece
        return first // out_cols, lax.rem(first, out_cols) // piece

    def t_copy_out(k, h):
        j, s = home(h)
        return remote(t_out.at[h], t_in.at[s, c], tn_s.at[h], tn_r.at[s], k * 2 + parity, j)

    def g_copy(k, h):
        j, s = home(h)
        return remote(g_out.at[k, h], g_in.at[s, c], g_s.at[h], g_r.at[s], k * 2 + parity, j)

    def scatter_pieces(make, own_in, own_out):
        for k in range(groups):
            for h in range(halves):
                j, s = home(h)
                here = jnp.logical_and(group == k, c == j)

                @pl.when(jnp.logical_not(here))
                def _():
                    make(k, h).start()

                @pl.when(here)
                def _():
                    own_in[s, c] = own_out(k, h)

    def drain_pieces(like, send):
        for h in range(halves):
            j, _ = home(h)

            @pl.when(c == j)
            def _():
                sent(like(groups - 1), send.at[h])

            @pl.when(c != j)
            def _():
                sent(like(groups), send.at[h])

    def receive_pieces(buf, recv):
        for s in range(slots):
            source = (c * out_cols + s * piece) // shared

            @pl.when(group == source)
            def _():
                received(buf.at[s, : n - 1], recv.at[s])

            @pl.when(group != source)
            def _():
                received(buf.at[s], recv.at[s])

    def turn_targets(side):
        t = t_all[side].T
        t_turned[side] = t
        t = t.astype(F32)
        norms[side] = jnp.broadcast_to(jnp.sum(t * t, axis=0, keepdims=True), (8, own_targets))

    def turn(it, lag):
        return jnp.logical_and(it >= lag, it < pairs + lag)

    def step(it, _):
        @pl.when(it < pairs)
        def _():
            arrived(in_buf.at[it], load_sem.at[it])
            project((1 - core) * pairs + it, 0, wide_out, it, pair_out)
            project(core * pairs + it, 1, wide_own, it, mine)

            @pl.when(it == 0)
            def _():
                pl.semaphore_wait(barrier, 1 + levels + lower + upper_plane)
                t_copy.wait()
                remote(t_all.at[parity], t_all.at[parity], mate_s, mate_r, mate, c).start()
                if far > 0:
                    tell()

            pair_copy(it).start()
            wide_copy(it).start()

        @pl.when(turn(it, 1))
        def _():
            i = it - 1
            pair_copy(i).wait_recv()
            for part in range(PARTS):
                comb[i, 0, part] = (mine[i, part].astype(F32) + pair_in[i, part].astype(F32)).astype(BF16)
                step_copy(i, 0, part).start()

        for level in range(1, levels):

            @pl.when(turn(it, 1 + LAG * level))
            def _():
                i = it - (1 + LAG * level)
                received(step_in.at[i, level - 1], step_r.at[i, level - 1])
                for part in range(PARTS):
                    both = comb[i, level - 1, part].astype(F32) + step_in[i, level - 1, part].astype(F32)
                    comb[i, level, part] = both.astype(BF16)
                    step_copy(i, level, part).start()

        @pl.when(turn(it, last_lag))
        def _():
            i = it - last_lag
            wide_copy(i).wait_recv()
            received(step_in.at[i, levels - 1], step_r.at[i, levels - 1])
            whole = []
            for part in range(PARTS):
                both = comb[i, levels - 1, part].astype(F32) + step_in[i, levels - 1, part].astype(F32)
                whole.append(both.astype(BF16))
            g = jnp.concatenate(whole, axis=1)
            left = mm(g, wide_own[i, :, :256]) + mm(g, wide_in[i, :, :256])
            right = mm(g[3 * rc :], wide_own[i, :, 256:]) + mm(g[3 * rc :], wide_in[i, :, 256:])
            b, place = i // per, lax.rem(i, per)
            found[place, : 2 * rc] = left[: 2 * rc, :128]
            found[place, 2 * rc : 3 * rc] = left[2 * rc : 3 * rc, 128:]
            found[place, 3 * rc :] = right

            @pl.when(place == per - 1)
            def _():
                for q in range(n):
                    feat_out[b, q] = jnp.concatenate(
                        [found[p, q * rows : (q + 1) * rows] for p in range(per)], axis=0
                    ).astype(BF16)
                for r in range(1, n):
                    feat_copy(b, r).start()

        if far > 0:

            @pl.when(jnp.logical_and(lax.rem(it, 2) == 0, jnp.logical_and(it >= 2, it <= 2 * far)))
            def _():
                hear()

                @pl.when(it < 2 * far)
                def _():
                    tell()

        @pl.when(it == pairs)
        def _():
            turn_targets(parity)

        @pl.when(it == pairs + 4)
        def _():
            received(t_all.at[1 - parity], mate_r)
            turn_targets(1 - parity)

        return 0

    lax.fori_loop(0, max(pairs + last_lag, 2 * far + 1), step, 0)

    arrived(m_ref, fixed_sem.at[5])
    m1 = jnp.concatenate([m_ref[0, c]] * per, axis=0)
    m2 = jnp.concatenate([m_ref[1, c]] * per, axis=0)

    norm = jnp.concatenate([norms[0], norms[1]], axis=1)
    for h in range(halves):
        t_out[h] = norm[:, h * piece : (h + 1) * piece]

    def keep(b, i, k, u):
        u = u.astype(F32)
        for p in range(per):
            u_f32[i * examples + k * pairs + b * per + p] = u[p * rows : (p + 1) * rows]

    for b in range(batches):
        sums = [feat_out[b, c].astype(F32), None]
        received(feat_in.at[b, 1:], feat_r.at[b])
        for r in range(1, n):
            f = feat_in[b, r].astype(F32)
            sums[r % 2] = f if sums[r % 2] is None else sums[r % 2] + f
        for f, k in ((sums[0], core), (sums[1], 1 - core)):
            new = (0.9 * m1 + 0.1 * f) / (jnp.sqrt(0.999 * m2 + 0.001 * f * f) + 1e-08)
            u = new.astype(BF16)
            u_all[b, group, k] = u
            keep(b, group, k, u)
        for r in range(1, groups):
            u_copy(b, r, group).start()

    squares = None
    for r in range(rows):
        u = u_f32[pl.ds(group * examples, examples), r, :]
        squares = u * u if squares is None else squares + u * u
    sq_out[...] = squares
    for r in range(1, n):
        sq_copy(r).start()

    for b in range(batches):
        received(u_all.at[b, : groups - 1], u_r.at[b])
        for r in range(1, groups):
            source = lax.rem(group + groups - r, groups)
            for k in range(2):
                keep(b, source, k, u_all[b, source, k])
        if b == 0:
            scatter_pieces(t_copy_out, t_in, lambda k, h: t_out[h])

    u_rows = jnp.concatenate([u_f32[:, r, :].astype(BF16) for r in range(rows)], axis=1)
    dots = jnp.concatenate([mm(u_rows, t_turned[side]) for side in range(2)], axis=1).astype(BF16)
    for k in range(groups):
        for h in range(halves):
            g_out[k, h] = dots[k * examples : (k + 1) * examples, h * piece : (h + 1) * piece]
    scatter_pieces(g_copy, g_in, lambda k, h: g_out[k, h])

    received(sq_in.at[1:], sq_r)
    for r in range(1, n):
        squares = squares + sq_in[r]
    row_scale = lax.rsqrt(jnp.sum(squares, axis=1, keepdims=True) + 1e-06) * math.sqrt(ranks * 128)
    receive_pieces(t_in, tn_r)
    column_scale = []
    for s in range(slots):
        norm = t_in[s, 0]
        for cc in range(1, n):
            norm = norm + t_in[s, cc]
        column_scale.append(lax.rsqrt(norm[:1] + 1e-06))
    receive_pieces(g_in, g_r)
    for s in range(slots):
        acc = g_in[s, 0].astype(F32)
        for cc in range(1, n):
            acc = acc + g_in[s, cc].astype(F32)
        out_ref[:, s * piece : (s + 1) * piece] = acc * row_scale * column_scale[s]

    sent(pair_out, send_sem.at[0])
    sent(wide_out, send_sem.at[1])
    sent(comb, send_sem.at[2])
    sent(feat_out.at[:, 1:], send_sem.at[3])
    sent(u_all.at[:, 1:], send_sem.at[4])
    sent(t_all.at[parity], mate_s)
    sent(sq_in.at[1:], send_sem.at[5])
    drain_pieces(lambda count: t_in.at[0, :count], tn_s)
    drain_pieces(lambda count: g_out.at[:count, 0], g_s)


def body(nd, n, x, q, v, lengths, reducing, expanding, width, sketch, m1, m2, targets):
    examples, seq, depth = x.shape
    ranks = 4 * sketch.shape[1]
    pairs, chips, rows = examples // 2, n // 2, ranks // n
    levels = chips.bit_length() - 1
    half = seq // 2
    per = max(1, 16 // rows)
    batches = pairs // per
    own_targets = targets.shape[0]
    out_cols = own_targets * nd // n
    shared, groups = 2 * own_targets, nd // 2
    piece = min(shared, out_cols)
    halves, slots = shared // piece, out_cols // piece
    dma = pltpu.SemaphoreType.DMA
    anywhere = pl.BlockSpec(memory_space=pl.ANY)
    vmem = pl.BlockSpec(memory_space=pltpu.VMEM)
    return pl.pallas_call(
        functools.partial(kernel, nd, n),
        out_shape=pltpu.VMEM((examples, out_cols), F32),
        in_specs=[anywhere] * 11,
        out_specs=vmem,
        scratch_shapes=[
            pltpu.VMEM((pairs, 2, 3, seq, depth), BF16),
            pltpu.VMEM((2, *targets.shape), BF16),
            pltpu.VMEM((2, *targets.shape[::-1]), BF16),
            pltpu.VMEM((2, 8, own_targets), F32),
            pltpu.SMEM((examples,), jnp.int32),
            pltpu.VMEM(sketch.shape[::-1], BF16),
            pltpu.VMEM((2, n, rows, 128), F32),
            pltpu.VMEM(reducing.shape, BF16),
            pltpu.VMEM(expanding.shape, BF16),
            pltpu.VMEM((3, depth, 256), BF16),
            pltpu.VMEM((pairs, seq, 384), BF16),
            pltpu.VMEM((pairs, seq, 384), BF16),
            pltpu.VMEM((pairs, seq, 384), BF16),
            pltpu.VMEM((pairs, PARTS, ranks, half), BF16),
            pltpu.VMEM((pairs, PARTS, ranks, half), BF16),
            pltpu.VMEM((pairs, PARTS, ranks, half), BF16),
            pltpu.VMEM((pairs, levels, PARTS, ranks, half), BF16),
            pltpu.VMEM((pairs, levels, PARTS, ranks, half), BF16),
            pltpu.VMEM((per, ranks, 128), F32),
            pltpu.VMEM((batches, n, per * rows, 128), BF16),
            pltpu.VMEM((batches, n, per * rows, 128), BF16),
            pltpu.VMEM((batches, groups, 2, per * rows, 128), BF16),
            pltpu.VMEM((groups * examples, rows, 128), F32),
            pltpu.VMEM((examples, 128), F32),
            pltpu.VMEM((n, examples, 128), F32),
            pltpu.VMEM((halves, 8, piece), F32),
            pltpu.VMEM((slots, n, 8, piece), F32),
            pltpu.VMEM((groups, halves, examples, piece), BF16),
            pltpu.VMEM((slots, n, examples, piece), BF16),
            dma((pairs,)),
            dma,
            dma((6,)),
            dma((6,)),
            dma((pairs,)),
            dma((pairs,)),
            dma((pairs, levels)),
            dma((batches,)),
            dma((batches,)),
            dma,
            dma((halves,)),
            dma((slots,)),
            dma((halves,)),
            dma((slots,)),
            dma,
            dma,
            pltpu.SemaphoreType.REGULAR,
            pltpu.SemaphoreType.REGULAR,
        ],
        compiler_params=pltpu.CompilerParams(
            collective_id=0, has_side_effects=True, vmem_limit_bytes=56 * 1024 * 1024
        ),
    )(
        x,
        q,
        v,
        lengths,
        reducing,
        expanding,
        width,
        sketch.T,
        m1.reshape(n, rows, 128),
        m2.reshape(n, rows, 128),
        targets,
    )


def solution(mesh):
    placed = (
        P("dp", None, "tp"),
        P("dp", None, "tp"),
        P("dp", None, "tp"),
        P("dp"),
        P(None, "tp", None),
        P(None, None, "tp"),
        P(None, "tp", None),
        P(),
        P(),
        P(),
        P("dp", "tp"),
    )
    names = mesh.axis_names
    order = (mesh.shape["dp"], mesh.shape["tp"])
    run = functools.partial(body, *order)
    assert set(names) == {"dp", "tp"}
    return jax.shard_map(run, mesh=mesh, in_specs=placed, out_specs=P("dp", "tp"), check_vma=False)
```

```python
import functools
import math

import jax
import jax.numpy as jnp
from jax import lax
from jax.experimental import pallas as pl
from jax.experimental.pallas import tpu as pltpu
from jax.sharding import PartitionSpec as P

MESH = pl.DeviceIdType.MESH
F32 = jnp.float32
BF16 = jnp.bfloat16
PARTS = 2
LAG = 3
WIDE = 4
EARLY = 4


def mm(a, b, ca=1, cb=0):
    return lax.dot_general(a, b, (((ca,), (cb,)), ((), ())), preferred_element_type=F32)


def kernel(
    nd,
    n,
    x_hbm,
    q_hbm,
    v_hbm,
    len_hbm,
    red_hbm,
    exp_hbm,
    width_hbm,
    sketch_hbm,
    m1_hbm,
    m2_hbm,
    t_hbm,
    out_ref,
    in_buf,
    t_all,
    t_turned,
    norms,
    len_ref,
    sketch_ref,
    m_ref,
    red_ref,
    exp_ref,
    w_buf,
    wide_out,
    wide_in,
    wide_own,
    pair_out,
    pair_in,
    mine,
    comb,
    step_in,
    g_all,
    found,
    feat_out,
    feat_in,
    u_all,
    u_f32,
    sq_out,
    sq_in,
    t_out,
    t_in,
    g_out,
    g_in,
    load_sem,
    t_sem,
    fixed_sem,
    send_sem,
    pair_r,
    wide_r,
    step_r,
    join_r,
    feat_r,
    u_r,
    sq_r,
    tn_s,
    tn_r,
    g_s,
    g_r,
    mate_s,
    mate_r,
    low_sem,
    high_sem,
):
    d = lax.axis_index("dp")
    c = lax.axis_index("tp")
    chips = n // 2
    levels = chips.bit_length() - 1
    chip, core = c // 2, lax.rem(c, 2)
    partner = chip * 2 + 1 - core
    pairs, _, _, seq, depth = in_buf.shape
    examples = pairs * 2
    rc = sketch_ref.shape[0]
    ranks = 4 * rc
    half = seq // 2
    rows = ranks // n
    batches, _, tile, _ = feat_out.shape
    per = tile // rows
    parity, mate = lax.rem(d, 2), d + 1 - 2 * lax.rem(d, 2)
    own_targets = t_all.shape[1]
    group, groups, shared = d // 2, nd // 2, 2 * own_targets
    out_cols = out_ref.shape[1]
    piece = min(shared, out_cols)
    halves = shared // piece
    slots = out_cols // piece
    far = nd - 3
    last_lag = 1 + LAG * levels
    early = EARLY if levels == 2 else 0

    def remote(src, dst, send, recv, dd, cc):
        return pltpu.make_async_remote_copy(
            src_ref=src, dst_ref=dst, send_sem=send, recv_sem=recv, device_id={"dp": dd, "tp": cc}, device_id_type=MESH
        )

    def arrived(block, sem):
        pltpu.make_async_copy(block, block, sem).wait()

    def received(block, sem):
        remote(block, block, sem, sem, d, partner).wait_recv()

    def sent(block, sem):
        remote(block, block, sem, sem, d, partner).wait_send()

    def signal(sem, dd, cc):
        pl.semaphore_signal(sem, inc=1, device_id={"dp": dd, "tp": cc}, device_id_type=MESH)

    def across(bit):
        m = 1 << bit
        return (chip + m * (1 - 2 * lax.rem(chip // m, 2))) * 2 + core

    barrier = pltpu.get_barrier_semaphore()
    signal(barrier, d, partner)
    for bit in range(levels):
        signal(barrier, d, across(bit))

    @pl.when(d > 0)
    def _():
        signal(barrier, d - 1, c)

    @pl.when(d < nd - 1)
    def _():
        signal(barrier, d + 1, c)

    fixed = [
        pltpu.make_async_copy(src, dst, fixed_sem.at[j])
        for src, dst, j in [(sketch_hbm, sketch_ref, 0), (red_hbm, red_ref, 1), (exp_hbm, exp_ref, 2)]
        + [(width_hbm.at[min(j, 1)], w_buf.at[j, :, 128:], 3) for j in range(3)]
        + [(len_hbm, len_ref, 4), (m1_hbm, m_ref.at[0], 5), (m2_hbm, m_ref.at[1], 5)]
    ]
    for copy in fixed:
        copy.start()

    def start_loads(i, _):
        for side in range(2):
            e = (core if side else 1 - core) * pairs + i
            for j, src in enumerate((x_hbm, q_hbm, v_hbm)):
                pltpu.make_async_copy(src.at[e], in_buf.at[i, side, j], load_sem.at[i]).start()
        return 0

    t_copy = pltpu.make_async_copy(t_hbm, t_all.at[parity], t_sem)
    t_copy.start()
    lax.fori_loop(0, pairs, start_loads, 0)

    fixed[0].wait()
    sketch = sketch_ref[...]

    def placed(slot):
        row = lax.broadcasted_iota(jnp.int32, (rc, 128), 0)
        col = lax.broadcasted_iota(jnp.int32, (rc, 128), 1)
        here = jnp.logical_or(col == row + slot * rc, col == row + slot * rc + ranks)
        return mm(sketch, jnp.where(here, 1.0, 0.0).astype(BF16), 0, 0).astype(BF16)

    spread = [placed(slot) for slot in range(4)]
    fixed[1].wait()
    w_buf[0, :, :128] = (mm(red_ref[0], spread[2]) + mm(red_ref[1], spread[3])).astype(BF16)
    fixed[2].wait()
    w_buf[1, :, :128] = mm(exp_ref[0], spread[0], 0, 0).astype(BF16)
    w_buf[2, :, :128] = mm(exp_ref[1], spread[1], 0, 0).astype(BF16)
    arrived(w_buf.at[:, :, 128:], fixed_sem.at[3])
    fixed[6].wait()

    lower, upper_plane = jnp.where(d > 0, 1, 0), jnp.where(d < nd - 1, 1, 0)

    def tell():
        @pl.when(d > 0)
        def _():
            signal(high_sem, d - 1, c)

        @pl.when(d < nd - 1)
        def _():
            signal(low_sem, d + 1, c)

    def hear():
        @pl.when(d > 0)
        def _():
            pl.semaphore_wait(low_sem, 1)

        @pl.when(d < nd - 1)
        def _():
            pl.semaphore_wait(high_sem, 1)

    def project(e, side, wide, i, out):
        row = lax.broadcasted_iota(jnp.int32, (half, 128), 0)
        upper = lax.broadcasted_iota(jnp.int32, (half, 128), 1) >= ranks
        live = jnp.where(upper, row + half, row) < len_ref[e]
        for k in range(half // 128):
            sums = []
            for late in range(2):
                span = pl.ds(late * half + k * 128, 128)
                narrow = None
                for j in range(3):
                    res = mm(in_buf[i, side, j, span], w_buf[j])
                    wide[i, span, j * 128 : (j + 1) * 128] = res[:, 128:].astype(BF16)
                    narrow = res[:, :128] if narrow is None else narrow + res[:, :128]
                sums.append(narrow)
            packed = jnp.where(upper[:128], sums[1], sums[0])
            packed = jnp.where(live[k * 128 : (k + 1) * 128], packed, 0.0).astype(BF16)
            out[i, :, :, :, k * 128 : (k + 1) * 128] = packed.T.reshape(PARTS, 2, ranks // 2, 128)

    def pair_copy(i):
        return remote(pair_out.at[i], pair_in.at[i], send_sem.at[0], pair_r.at[i], d, partner)

    def wide_copy(i):
        return remote(wide_out.at[i], wide_in.at[i], send_sem.at[1], wide_r.at[i // WIDE], d, partner)

    def step_copy(i, level, part):
        return remote(
            comb.at[i, level, part],
            step_in.at[i, level, part],
            send_sem.at[2],
            step_r.at[i, level],
            d,
            across((level + part) % levels),
        )

    def kept(part):
        return lax.rem(chip // (1 << part % levels), 2)

    def split_copy(i, stage, part):
        near, other = part % levels, (part + 1) % levels
        k = kept(part)
        if stage == 0:
            src, dst = comb.at[i, 0, part, 1 - k], step_in.at[i, 0, part, 1 - k]
            return remote(src, dst, send_sem.at[6], step_r.at[i, 0], d, across(near))
        if stage == 1:
            src, dst = comb.at[i, 1, part, k], step_in.at[i, 1, part, k]
            return remote(src, dst, send_sem.at[6], step_r.at[i, 1], d, across(other))
        return remote(g_all.at[i, part, k], g_all.at[i, part, k], send_sem.at[7], join_r.at[i], d, across(near))

    def feat_copy(b, r):
        to = lax.rem(c + r, n)
        return remote(feat_out.at[b, to], feat_in.at[b, r], send_sem.at[3], feat_r.at[b], d, to)

    def u_copy(b, r, place):
        to = lax.rem(group + r, groups) * 2 + parity
        return remote(u_all.at[b, place], u_all.at[b, place], send_sem.at[4], u_r.at[b], to, c)

    def sq_copy(r):
        to = lax.rem(c + r, n)
        return remote(sq_out, sq_in.at[r], send_sem.at[5], sq_r, d, to)

    def home(h):
        first = group * shared + h * piece
        return first // out_cols, lax.rem(first, out_cols) // piece

    def t_copy_out(k, h):
        j, s = home(h)
        return remote(t_out.at[h], t_in.at[s, c], tn_s, tn_r.at[s], k * 2 + parity, j)

    def g_copy(k, h):
        j, s = home(h)
        return remote(g_out.at[k, h], g_in.at[s, c], g_s, g_r.at[s], k * 2 + parity, j)

    def scatter_pieces(make, own_in, own_out):
        for k in range(groups):
            for h in range(halves):
                j, s = home(h)
                here = jnp.logical_and(group == k, c == j)

                @pl.when(jnp.logical_not(here))
                def _():
                    make(k, h).start()

                @pl.when(here)
                def _():
                    own_in[s, c] = own_out(k, h)

    def drain_pieces(block, send):
        here = home(0)[0] == c
        for h in range(1, halves):
            here = jnp.logical_or(here, home(h)[0] == c)

        @pl.when(here)
        def _():
            sent(block.at[: groups * halves - 1], send)

        @pl.when(jnp.logical_not(here))
        def _():
            sent(block.at[: groups * halves], send)

    def receive_pieces(buf, recv):
        for s in range(slots):
            source = (c * out_cols + s * piece) // shared

            @pl.when(group == source)
            def _():
                received(buf.at[s, : n - 1], recv.at[s])

            @pl.when(group != source)
            def _():
                received(buf.at[s], recv.at[s])

    def turn_targets(side):
        t = t_all[side].T
        t_turned[side] = t
        t = t.astype(F32)
        norms[side] = jnp.broadcast_to(jnp.sum(t * t, axis=0, keepdims=True), (8, own_targets))

    def turn(it, lag, first=0, stop=pairs):
        return jnp.logical_and(it >= first + lag, it < stop + lag)

    def plus(a, b):
        return (a.astype(F32) + b.astype(F32)).astype(BF16)

    def features(i):
        @pl.when(lax.rem(i, WIDE) == 0)
        def _():
            received(wide_in.at[pl.ds(i, WIDE)], wide_r.at[i // WIDE])

        g = jnp.concatenate([g_all[i, part].reshape(ranks, half) for part in range(PARTS)], axis=1)
        left = mm(g, wide_own[i, :, :256]) + mm(g, wide_in[i, :, :256])
        right = mm(g[3 * rc :], wide_own[i, :, 256:]) + mm(g[3 * rc :], wide_in[i, :, 256:])
        b, place = i // per, lax.rem(i, per)
        found[b, place, : 2 * rc] = left[: 2 * rc, :128]
        found[b, place, 2 * rc : 3 * rc] = left[2 * rc : 3 * rc, 128:]
        found[b, place, 3 * rc :] = right

        @pl.when(place == per - 1)
        def _():
            for q in range(n):
                feat_out[b, q] = jnp.concatenate(
                    [found[b, p, q * rows : (q + 1) * rows] for p in range(per)], axis=0
                ).astype(BF16)
            for r in range(1, n):
                feat_copy(b, r).start()

    def step(it, _):
        @pl.when(it < pairs)
        def _():
            arrived(in_buf.at[it], load_sem.at[it])
            project((1 - core) * pairs + it, 0, wide_out, it, pair_out)
            project(core * pairs + it, 1, wide_own, it, mine)

            @pl.when(it == 0)
            def _():
                pl.semaphore_wait(barrier, 1 + levels + lower + upper_plane)
                t_copy.wait()
                remote(t_all.at[parity], t_all.at[parity], mate_s, mate_r, mate, c).start()
                if far > 0:
                    tell()

            pair_copy(it).start()
            wide_copy(it).start()

        @pl.when(turn(it, 1))
        def _():
            i = it - 1
            pair_copy(i).wait_recv()
            if early:

                @pl.when(i < early)
                def _():
                    for part in range(PARTS):
                        comb[i, 0, part] = plus(mine[i, part], pair_in[i, part])
                        split_copy(i, 0, part).start()

            @pl.when(i >= early)
            def _():
                for part in range(PARTS):
                    comb[i, 0, part] = plus(mine[i, part], pair_in[i, part])
                    step_copy(i, 0, part).start()

        for level in range(1, levels):

            @pl.when(turn(it, 1 + LAG * level, early))
            def _():
                i = it - (1 + LAG * level)
                received(step_in.at[i, level - 1], step_r.at[i, level - 1])
                for part in range(PARTS):
                    comb[i, level, part] = plus(comb[i, level - 1, part], step_in[i, level - 1, part])
                    step_copy(i, level, part).start()

        if early:

            @pl.when(turn(it, 1 + LAG, 0, early))
            def _():
                i = it - (1 + LAG)
                received(step_in.at[i, 0, :, 0], step_r.at[i, 0])
                for part in range(PARTS):
                    k = kept(part)
                    comb[i, 1, part, k] = plus(comb[i, 0, part, k], step_in[i, 0, part, k])
                    split_copy(i, 1, part).start()

            @pl.when(turn(it, 1 + 2 * LAG, 0, early))
            def _():
                i = it - (1 + 2 * LAG)
                received(step_in.at[i, 1, :, 0], step_r.at[i, 1])
                for part in range(PARTS):
                    k = kept(part)
                    g_all[i, part, k] = plus(comb[i, 1, part, k], step_in[i, 1, part, k])
                    split_copy(i, 2, part).start()

        @pl.when(turn(it, last_lag, early))
        def _():
            i = it - last_lag
            received(step_in.at[i, levels - 1], step_r.at[i, levels - 1])
            for part in range(PARTS):
                g_all[i, part] = plus(comb[i, levels - 1, part], step_in[i, levels - 1, part])
            features(i)

        if early:

            @pl.when(turn(it, 1 + 3 * LAG, 0, early))
            def _():
                i = it - (1 + 3 * LAG)
                received(g_all.at[i, :, 0], join_r.at[i])
                features(i)

        if far > 0:

            @pl.when(jnp.logical_and(lax.rem(it, 2) == 0, jnp.logical_and(it >= 2, it <= 2 * far)))
            def _():
                hear()

                @pl.when(it < 2 * far)
                def _():
                    tell()

        @pl.when(it == pairs)
        def _():
            turn_targets(parity)

        @pl.when(it == pairs + 4)
        def _():
            received(t_all.at[1 - parity], mate_r)
            turn_targets(1 - parity)

        return 0

    lax.fori_loop(0, max(pairs + last_lag, early + 1 + 3 * LAG, 2 * far + 1), step, 0)

    arrived(m_ref, fixed_sem.at[5])
    m1 = jnp.concatenate([m_ref[0, c]] * per, axis=0)
    m2 = jnp.concatenate([m_ref[1, c]] * per, axis=0)

    norm = jnp.concatenate([norms[0], norms[1]], axis=1)
    for h in range(halves):
        t_out[h] = norm[:, h * piece : (h + 1) * piece]

    def keep(b, i, k, u):
        u = u.astype(F32)
        for p in range(per):
            u_f32[i * examples + k * pairs + b * per + p] = u[p * rows : (p + 1) * rows]

    for b in range(batches):
        sums = [feat_out[b, c].astype(F32), None]
        received(feat_in.at[b, 1:], feat_r.at[b])
        for r in range(1, n):
            f = feat_in[b, r].astype(F32)
            sums[r % 2] = f if sums[r % 2] is None else sums[r % 2] + f
        for f, k in ((sums[0], core), (sums[1], 1 - core)):
            new = (0.9 * m1 + 0.1 * f) / (jnp.sqrt(0.999 * m2 + 0.001 * f * f) + 1e-08)
            u = new.astype(BF16)
            u_all[b, group, k] = u
        for r in range(1, groups):
            u_copy(b, r, group).start()
        for k in range(2):
            keep(b, group, k, u_all[b, group, k])

    squares = None
    for r in range(rows):
        u = u_f32[pl.ds(group * examples, examples), r, :]
        squares = u * u if squares is None else squares + u * u
    sq_out[...] = squares
    for r in range(1, n):
        sq_copy(r).start()

    for b in range(batches):
        received(u_all.at[b, : groups - 1], u_r.at[b])
        for r in range(1, groups):
            source = lax.rem(group + groups - r, groups)
            for k in range(2):
                keep(b, source, k, u_all[b, source, k])
        if b == 0:
            scatter_pieces(t_copy_out, t_in, lambda k, h: t_out[h])

    u_rows = jnp.concatenate([u_f32[:, r, :].astype(BF16) for r in range(rows)], axis=1)
    dots = jnp.concatenate([mm(u_rows, t_turned[side]) for side in range(2)], axis=1).astype(BF16)
    for k in range(groups):
        for h in range(halves):
            g_out[k, h] = dots[k * examples : (k + 1) * examples, h * piece : (h + 1) * piece]
    scatter_pieces(g_copy, g_in, lambda k, h: g_out[k, h])

    received(sq_in.at[1:], sq_r)
    for r in range(1, n):
        squares = squares + sq_in[r]
    row_scale = lax.rsqrt(jnp.sum(squares, axis=1, keepdims=True) + 1e-06) * math.sqrt(ranks * 128)
    receive_pieces(t_in, tn_r)
    column_scale = []
    for s in range(slots):
        norm = t_in[s, 0]
        for cc in range(1, n):
            norm = norm + t_in[s, cc]
        column_scale.append(lax.rsqrt(norm[:1] + 1e-06))
    receive_pieces(g_in, g_r)
    for s in range(slots):
        acc = g_in[s, 0].astype(F32)
        for cc in range(1, n):
            acc = acc + g_in[s, cc].astype(F32)
        out_ref[:, s * piece : (s + 1) * piece] = acc * row_scale * column_scale[s]

    sent(pair_out, send_sem.at[0])
    sent(wide_out, send_sem.at[1])
    sent(comb.at[early:], send_sem.at[2])
    if early:
        sent(comb.at[:early, :, :, 0], send_sem.at[6])
        sent(g_all.at[:early, :, 0], send_sem.at[7])
    sent(feat_out.at[:, 1:], send_sem.at[3])
    sent(u_all.at[:, 1:], send_sem.at[4])
    sent(t_all.at[parity], mate_s)
    sent(sq_in.at[1:], send_sem.at[5])
    drain_pieces(t_in.at[0], tn_s)
    drain_pieces(g_in.at[0], g_s)


def body(nd, n, x, q, v, lengths, reducing, expanding, width, sketch, m1, m2, targets):
    examples, seq, depth = x.shape
    ranks = 4 * sketch.shape[1]
    pairs, chips, rows = examples // 2, n // 2, ranks // n
    levels = chips.bit_length() - 1
    half = seq // 2
    per = max(1, 16 // rows)
    batches = pairs // per
    own_targets = targets.shape[0]
    out_cols = own_targets * nd // n
    shared, groups = 2 * own_targets, nd // 2
    piece = min(shared, out_cols)
    halves, slots = shared // piece, out_cols // piece
    dma = pltpu.SemaphoreType.DMA
    anywhere = pl.BlockSpec(memory_space=pl.ANY)
    vmem = pl.BlockSpec(memory_space=pltpu.VMEM)
    return pl.pallas_call(
        functools.partial(kernel, nd, n),
        out_shape=pltpu.VMEM((examples, out_cols), F32),
        in_specs=[anywhere] * 11,
        out_specs=vmem,
        scratch_shapes=[
            pltpu.VMEM((pairs, 2, 3, seq, depth), BF16),
            pltpu.VMEM((2, *targets.shape), BF16),
            pltpu.VMEM((2, *targets.shape[::-1]), BF16),
            pltpu.VMEM((2, 8, own_targets), F32),
            pltpu.SMEM((examples,), jnp.int32),
            pltpu.VMEM(sketch.shape[::-1], BF16),
            pltpu.VMEM((2, n, rows, 128), F32),
            pltpu.VMEM(reducing.shape, BF16),
            pltpu.VMEM(expanding.shape, BF16),
            pltpu.VMEM((3, depth, 256), BF16),
            pltpu.VMEM((pairs, seq, 384), BF16),
            pltpu.VMEM((pairs, seq, 384), BF16),
            pltpu.VMEM((pairs, seq, 384), BF16),
            pltpu.VMEM((pairs, PARTS, 2, ranks // 2, half), BF16),
            pltpu.VMEM((pairs, PARTS, 2, ranks // 2, half), BF16),
            pltpu.VMEM((pairs, PARTS, 2, ranks // 2, half), BF16),
            pltpu.VMEM((pairs, levels, PARTS, 2, ranks // 2, half), BF16),
            pltpu.VMEM((pairs, levels, PARTS, 2, ranks // 2, half), BF16),
            pltpu.VMEM((pairs, PARTS, 2, ranks // 2, half), BF16),
            pltpu.VMEM((batches, per, ranks, 128), F32),
            pltpu.VMEM((batches, n, per * rows, 128), BF16),
            pltpu.VMEM((batches, n, per * rows, 128), BF16),
            pltpu.VMEM((batches, groups, 2, per * rows, 128), BF16),
            pltpu.VMEM((groups * examples, rows, 128), F32),
            pltpu.VMEM((examples, 128), F32),
            pltpu.VMEM((n, examples, 128), F32),
            pltpu.VMEM((halves, 8, piece), F32),
            pltpu.VMEM((slots, n, 8, piece), F32),
            pltpu.VMEM((groups, halves, examples, piece), BF16),
            pltpu.VMEM((slots, n, examples, piece), BF16),
            dma((pairs,)),
            dma,
            dma((6,)),
            dma((8,)),
            dma((pairs,)),
            dma((pairs // WIDE,)),
            dma((pairs, levels)),
            dma((EARLY,)),
            dma((batches,)),
            dma((batches,)),
            dma,
            dma,
            dma((slots,)),
            dma,
            dma((slots,)),
            dma,
            dma,
            pltpu.SemaphoreType.REGULAR,
            pltpu.SemaphoreType.REGULAR,
        ],
        compiler_params=pltpu.CompilerParams(
            collective_id=0, has_side_effects=True, vmem_limit_bytes=56 * 1024 * 1024
        ),
    )(
        x,
        q,
        v,
        lengths,
        reducing,
        expanding,
        width,
        sketch.T,
        m1.reshape(n, rows, 128),
        m2.reshape(n, rows, 128),
        targets,
    )


def solution(mesh):
    placed = (
        P("dp", None, "tp"),
        P("dp", None, "tp"),
        P("dp", None, "tp"),
        P("dp"),
        P(None, "tp", None),
        P(None, None, "tp"),
        P(None, "tp", None),
        P(),
        P(),
        P(),
        P("dp", "tp"),
    )
    names = mesh.axis_names
    order = (mesh.shape["dp"], mesh.shape["tp"])
    run = functools.partial(body, *order)
    assert set(names) == {"dp", "tp"}
    return jax.shard_map(run, mesh=mesh, in_specs=placed, out_specs=P("dp", "tp"), check_vma=False)
```
